512 devices in a mesh: chain: 64 (over y, x, core), cols: 8 (over z).
Axes of the slice: x: 4, y: 8, z: 8, core: 2. Of those that a mesh axis runs over, the one named last changes fastest.
Arguments:
- start_vectors: float32 [1024, 256, 256], P('chain', 'cols'), may hold values from -6 to 6
- factors: float32 [1024, 256, 256], P('chain', 'cols'), may hold values from -1.2 to 1.2, as said below
Outputs:
- vectors: float32 [1024, 256, 256], P('chain', 'cols')
- log_growth: float32 [256], P('cols')
The draws below stay inside these ranges and needn't reach their ends.
Inputs may be any that keep to these rules, and one draw needn't show every extreme that they name: `factors`: the factor blocks of the shifted operator; every product of consecutive factor blocks is bounded.
All inputs are finite; a program needn't handle non-finite values.
Results may differ from the reference program's by a relative error of at most 0.0003.
Values sent between devices are 32-bit elements; how exact they have to be, the bound alone decides.
No kernel may reach another device: no remote copies, remote signals or barrier semaphores. Data moves between devices by JAX's collectives and lax.ppermute only.
A program may use at most 128 MiB of HBM per device.

```python
import math
import jax
import jax.numpy as jnp
from jax import lax

BLOCK = 256
VECTORS = 256
BLOCK_ROW_COUNT = 1024


def draw_factors(key, part):
    rate_key = jax.random.fold_in(key, 11)
    spread_key = jax.random.fold_in(key, 12)
    spike_key = jax.random.fold_in(key, 13)
    keep_key = jax.random.fold_in(key, 14)
    noise_key = jax.random.fold_in(key, 15)
    log_leak = jax.random.uniform(rate_key, (BLOCK,), jnp.float32, -3.3, -0.9)
    spread = jnp.exp(jax.random.uniform(spread_key, (BLOCK_ROW_COUNT, 1), jnp.float32, -0.7, 0.7))
    decay_factor = jnp.power(10.0, log_leak)[None, :] * spread
    spike_row_count = jax.random.randint(spike_key, (4,), 0, BLOCK_ROW_COUNT)
    spike_flags = jnp.any(jnp.arange(BLOCK_ROW_COUNT)[:, None] == spike_row_count[None, :], axis=1)
    retained_fraction = jax.random.uniform(keep_key, (BLOCK_ROW_COUNT, 1), jnp.float32, 0.5, 0.8)
    row_decay_factors = (1.0 - decay_factor) * jnp.where(spike_flags[:, None], retained_fraction, 1.0)
    mix_noise = jax.random.truncated_normal(noise_key, -4.0, 4.0, (BLOCK_ROW_COUNT, BLOCK, BLOCK), jnp.float32) * (0.25 / math.sqrt(BLOCK))
    mixing = (jnp.eye(BLOCK, dtype=jnp.float32)[None] + mix_noise) * (1.0 / math.sqrt(1.0625))
    return row_decay_factors[:, :, None] * mixing


def block_scale(own_key, extent, shards, least, top_value):
    factor_of = 1.0
    for position, blocks in shards:
        draws = jax.random.uniform(jax.random.fold_in(jax.random.fold_in(own_key, 6), position), (blocks,), jnp.float32, least / len(shards), top_value / len(shards))
        factor_of = factor_of * jnp.repeat(jnp.exp(draws), extent[position] // blocks).reshape((-1,) + (1,) * (len(extent) - 1 - position))
    return factor_of


def scatter_about(stream_key, shape, scale, reach, cuts=(), kind=jnp.bfloat16):
    level = block_scale(stream_key, shape, cuts, -0.22, 0.18) if cuts else 1.0
    array = jax.random.normal(stream_key, shape, jnp.float32) * scale * level
    return jnp.minimum(jnp.maximum(array, -reach), reach).astype(kind)


def setup_inputs(seed: int = 0) -> dict:
    splits = jax.random.split(jax.random.key(seed), 3)
    return {
        "start_vectors": scatter_about(splits[0], (BLOCK_ROW_COUNT, VECTORS, BLOCK), 1.0, 6.0, ((0, 64), (1, 8)), jnp.float32),
        "factors": draw_factors(jax.random.fold_in(splits[2], 71), 0),
    }


eps_value = 1e-06

def transform(matrix, vectors_in):
    return lax.dot_general(vectors_in, matrix, (((1,), (1,)), ((), ())), precision=lax.Precision.HIGHEST, preferred_element_type=vectors_in.dtype)

def solve_system(factors, right_side):
    zero_state = jnp.zeros(right_side.shape[1:], right_side.dtype)

    def forward_step(carried, element):
        matrix, source = element
        carried = transform(matrix, carried) + source
        return (carried, carried)

    def backward_step(carried, element):
        matrix, source = element
        carried = transform(matrix, source + carried)
        return (carried, carried)
    _, forward = lax.scan(forward_step, zero_state, (factors, right_side))
    _, solved = lax.scan(backward_step, zero_state, (factors, forward), reverse=True)
    return solved

def reference(start_vectors, factors):
    cell_count = BLOCK_ROW_COUNT * BLOCK
    first_solve = solve_system(factors, start_vectors)
    scale_one = jnp.sqrt(lax.optimization_barrier(jnp.sum(first_solve * first_solve, axis=(0, 2))) / cell_count + eps_value)
    second_solve = solve_system(factors, first_solve / scale_one[None, :, None])
    scale_two = jnp.sqrt(lax.optimization_barrier(jnp.sum(second_solve * second_solve, axis=(0, 2))) / cell_count + eps_value)
    return (second_solve / scale_two[None, :, None], jnp.log(scale_two))
```

```python
import functools

import jax
import jax.numpy as jnp
from jax import lax
from jax.experimental import pallas as pl
from jax.experimental.pallas import tpu as pltpu
from jax.sharding import Mesh, PartitionSpec as P

eps_value = 1e-06
VMEM_BYTES = 56 * 1024 * 1024


def split(value):
    high = value.astype(jnp.bfloat16)
    low = (value - high.astype(jnp.float32)).astype(jnp.bfloat16)
    return high, low


def apply_split(state, high, low):
    rows = state.shape[0]
    state_high, state_low = split(state)
    both = jnp.dot(
        jnp.concatenate([state_high, state_low], axis=0),
        high,
        preferred_element_type=jnp.float32,
    )
    return (both[:rows] + both[rows:]) + jnp.dot(
        state_high, low, preferred_element_type=jnp.float32
    )


def matmul(left, right):
    return jnp.dot(
        left, right, precision=lax.Precision.HIGHEST, preferred_element_type=jnp.float32
    )


def call(body, out_shapes, scratch, flops, *operands):
    vmem = pl.BlockSpec(memory_space=pltpu.VMEM)
    touched = sum(x.size * x.dtype.itemsize for x in (*operands, *out_shapes))
    return pl.pallas_call(
        body,
        out_shape=tuple(out_shapes),
        in_specs=[vmem] * len(operands),
        out_specs=tuple([vmem] * len(out_shapes)),
        scratch_shapes=scratch,
        compiler_params=pltpu.CompilerParams(vmem_limit_bytes=VMEM_BYTES),
        cost_estimate=pl.CostEstimate(flops=flops, bytes_accessed=touched, transcendentals=0),
    )(*operands)


def shape(*dims, dtype=jnp.float32):
    return jax.ShapeDtypeStruct(dims, dtype)


def prepare_body(factors, source, high, low, forward, prefix, suffix, ahead, behind):
    rows, width, _ = factors.shape
    count = source.shape[1]

    def turn(i, _):
        turned = factors[i].T
        high[i], low[i] = split(turned)
        return 0

    lax.fori_loop(0, rows, turn, 0)
    eye = (
        lax.broadcasted_iota(jnp.int32, (width, width), 0)
        == lax.broadcasted_iota(jnp.int32, (width, width), 1)
    ).astype(jnp.float32)
    ahead[:count] = jnp.zeros((count, width), jnp.float32)
    ahead[count:] = eye
    behind[...] = eye

    def step(i, _):
        j = rows - 1 - i
        moved = apply_split(ahead[...], high[i], low[i])
        back = apply_split(behind[...], high[j], low[j])
        state = moved[:count] + source[i]
        forward[i] = state
        prefix[i] = moved[count:]
        ahead[:count] = state
        ahead[count:] = moved[count:]
        suffix[j] = back
        behind[...] = back
        return 0

    lax.fori_loop(0, rows, step, 0)


def prepare(factors, source):
    rows, width, _ = factors.shape
    count = source.shape[1]
    square = (rows, width, width)
    return call(
        prepare_body,
        [
            shape(*square, dtype=jnp.bfloat16),
            shape(*square, dtype=jnp.bfloat16),
            shape(*source.shape),
            shape(*square),
            shape(*square),
        ],
        [pltpu.VMEM((count + width, width), jnp.float32), pltpu.VMEM((width, width), jnp.float32)],
        rows * 6 * (count + 2 * width) * width * width,
        factors,
        source,
    )


def couple_body(high, low, forward, prefix, suffix, first_end, cross, turn, behind, ahead):
    rows, count, width = forward.shape
    ahead[...] = jnp.zeros_like(ahead)
    behind[...] = jnp.zeros_like(behind)

    def step(i, _):
        j = rows - 1 - i
        entering = jnp.concatenate([forward[j], prefix[j]], axis=0) + behind[...]
        behind[...] = apply_split(entering, high[j], low[j])
        ahead[...] = apply_split(ahead[...], high[i], low[i]) + suffix[i]
        return 0

    lax.fori_loop(0, rows, step, 0)
    first_end[...] = behind[:count]
    cross[...] = behind[count:]
    turn[...] = ahead[...]


def couple(high, low, forward, prefix, suffix):
    rows, count, width = forward.shape
    return call(
        couple_body,
        [shape(count, width), shape(width, width), shape(width, width)],
        [pltpu.VMEM((count + width, width), jnp.float32), pltpu.VMEM((width, width), jnp.float32)],
        rows * 6 * (count + 2 * width) * width * width,
        high,
        low,
        forward,
        prefix,
        suffix,
    )


def sweep_body(reverse, high, low, source, entering, result):
    rows = source.shape[0]

    def step(i, state):
        if reverse:
            j = rows - 1 - i
            state = apply_split(source[j] + state, high[j], low[j])
        else:
            j = i
            state = apply_split(state, high[j], low[j]) + source[j]
        result[j] = state
        return state

    lax.fori_loop(0, rows, step, entering[...], unroll=2)


def sweep(high, low, source, entering, reverse):
    rows, count, width = source.shape
    return call(
        functools.partial(sweep_body, reverse),
        [shape(*source.shape)],
        [],
        rows * 6 * count * width * width,
        high,
        low,
        source,
        entering,
    )[0]


def exchange(value, level):
    size = lax.axis_size("chain")
    return lax.ppermute(value, "chain", [(i, i ^ (1 << level)) for i in range(size)])


def levels():
    return (lax.axis_size("chain") - 1).bit_length()


def upper_at(level):
    return (lax.axis_index("chain") >> level) & 1 == 1


def compose_levels(operator, reverse):
    passing, leading = [], []
    lead = None
    for level in range(levels()):
        after = ~upper_at(level) if reverse else upper_at(level)
        leading.append(lead)
        if level + 1 == levels():
            passing.append(None)
            break
        received = exchange(operator, level)
        first = jnp.where(after, received, operator)
        second = jnp.where(after, operator, received)
        passing.append(second)
        if lead is None:
            eye = jnp.eye(operator.shape[0], dtype=jnp.float32)
            lead = jnp.where(after, received, eye)
        else:
            lead = jnp.where(after, matmul(received, lead), lead)
        operator = matmul(first, second)
    return passing, leading


def scan_blocks(total, passing, leading, reverse):
    entering = jnp.zeros_like(total)
    for level in range(levels()):
        after = ~upper_at(level) if reverse else upper_at(level)
        received = exchange(total, level)
        lead = leading[level]
        carried = received if lead is None else matmul(received, lead)
        entering = jnp.where(after, entering + carried, entering)
        if level + 1 < levels():
            first = jnp.where(after, received, total)
            second = jnp.where(after, total, received)
            total = matmul(first, passing[level]) + second
    return entering


def norm_body(middle, suffix, entering, scale, result, squares):
    rows, count, width = middle.shape
    state_high, state_low = split(entering[...])
    stacked = jnp.concatenate([state_high, state_low], axis=0)
    divide = 1.0 / scale[...]

    def step(i, total):
        high, low = split(suffix[i])
        both = jnp.dot(stacked, high, preferred_element_type=jnp.float32)
        moved = (both[:count] + both[count:]) + jnp.dot(
            state_high, low, preferred_element_type=jnp.float32
        )
        value = (middle[i] + moved) * divide
        result[i] = value
        return total + value * value

    total = lax.fori_loop(0, rows, step, jnp.zeros((count, width), jnp.float32), unroll=2)
    squares[...] = jnp.broadcast_to(jnp.sum(total, axis=1, keepdims=True), squares.shape)


def finish(middle, suffix, entering, scale):
    rows, count, width = middle.shape
    return call(
        norm_body,
        [shape(*middle.shape), shape(count, 128)],
        [],
        rows * 6 * count * width * width,
        middle,
        suffix,
        entering,
        scale,
    )


def scale_body(vectors, scale, result):
    result[...] = vectors[...] * (1.0 / scale[...])[None]


def rescale(vectors, scale):
    return call(scale_body, [shape(*vectors.shape)], [], vectors.size, vectors, scale)[0]


def chain_total(value, groups):
    size = lax.axis_size("chain")
    for members in groups:
        n = len(members[0])
        copies = jnp.broadcast_to(value[None], (n, *value.shape))
        got = lax.all_to_all(copies, "chain", 0, 0, axis_index_groups=members, tiled=True)
        value = jnp.sum(got, axis=0)
    return value


def chain_groups():
    size = lax.axis_size("chain")
    inner = 1 << (levels() // 2)
    outer = size // inner
    near = [[g * inner + j for j in range(inner)] for g in range(outer)]
    far = [[g * inner + j for g in range(outer)] for j in range(inner)]
    return near, far


def shards(start_vectors, factors):
    rows, count, width = start_vectors.shape
    cell_count = rows * lax.axis_size("chain") * width
    groups = chain_groups()
    whole = lax.all_gather(factors, "cols", axis=1, tiled=True)
    high, low, forward, prefix, suffix = prepare(whole, start_vectors)
    first_end, cross, turn = couple(high, low, forward, prefix, suffix)
    ahead = compose_levels(prefix[rows - 1], False)
    behind = compose_levels(suffix[0], True)
    zero = jnp.zeros((count, width), jnp.float32)

    entering = scan_blocks(forward[rows - 1], *ahead, False)
    end = first_end + matmul(entering, cross)
    forward = sweep(high, low, start_vectors, entering, False)
    middle = sweep(high, low, forward, zero, True)
    middle_end = sweep(high, low, middle, zero, False)[rows - 1]

    entering = scan_blocks(end, *behind, True)
    end = middle_end + matmul(entering, turn)
    first_solve = sweep(high, low, forward, entering, True)
    squares = jnp.sum(first_solve * first_solve, axis=(0, 2))
    forward = sweep(high, low, first_solve, zero, False)
    middle_end = sweep(high, low, forward, zero, True)[0]

    entering = scan_blocks(end, *ahead, False)
    end = middle_end + matmul(entering, cross)
    forward = sweep(high, low, first_solve, entering, False)
    middle = sweep(high, low, forward, zero, True)

    entering = scan_blocks(end, *behind, True)
    padded = jnp.broadcast_to(squares[:, None], (count, 128))
    scale_one = jnp.sqrt(chain_total(padded, groups) / cell_count + eps_value)
    second, squares = finish(middle, suffix, entering, scale_one[:, :1])
    scale_two = jnp.sqrt(chain_total(squares, groups) / cell_count + eps_value)
    return rescale(second, scale_two[:, :1]), jnp.log(scale_two[:, 0])


def solution(mesh):
    return jax.shard_map(
        shards,
        mesh=mesh,
        in_specs=(P("chain", "cols", None), P("chain", "cols", None)),
        out_specs=(P("chain", "cols", None), P("cols")),
        check_vma=False,
    )
```

```python
import functools

import jax
import jax.numpy as jnp
from jax import lax
from jax.experimental import pallas as pl
from jax.experimental.pallas import tpu as pltpu
from jax.sharding import Mesh, PartitionSpec as P

eps_value = 1e-06
VMEM_BYTES = 56 * 1024 * 1024
CHAIN = ("outer", "inner")


def split(value):
    high = value.astype(jnp.bfloat16)
    low = (value - high.astype(jnp.float32)).astype(jnp.bfloat16)
    return high, low


def apply_split(state, high, low):
    rows = state.shape[0]
    state_high, state_low = split(state)
    both = jnp.dot(
        jnp.concatenate([state_high, state_low], axis=0),
        high,
        preferred_element_type=jnp.float32,
    )
    return (both[:rows] + both[rows:]) + jnp.dot(
        state_high, low, preferred_element_type=jnp.float32
    )


def matmul(left, right):
    return jnp.dot(
        left, right, precision=lax.Precision.HIGHEST, preferred_element_type=jnp.float32
    )


def call(body, out_shapes, scratch, flops, *operands, after=None, position=None):
    vmem = pl.BlockSpec(memory_space=pltpu.VMEM)
    touched = sum(x.size * x.dtype.itemsize for x in (*operands, *out_shapes))
    specs = [vmem] * len(operands)
    if position is not None:
        specs = [pl.BlockSpec(memory_space=pltpu.SMEM), *specs]
        operands = (position, *operands)
    kernel = body
    if after is not None:
        specs = [pl.BlockSpec(memory_space=pl.ANY), *specs]
        operands = (after, *operands)

        def kernel(_, *refs):
            body(*refs)

    return pl.pallas_call(
        kernel,
        out_shape=tuple(out_shapes),
        in_specs=specs,
        out_specs=tuple([vmem] * len(out_shapes)),
        scratch_shapes=scratch,
        compiler_params=pltpu.CompilerParams(vmem_limit_bytes=VMEM_BYTES),
        cost_estimate=pl.CostEstimate(flops=flops, bytes_accessed=touched, transcendentals=0),
    )(*operands)


def shape(*dims, dtype=jnp.float32):
    return jax.ShapeDtypeStruct(dims, dtype)


def prepare_body(factors, source, high, low, forward, prefix, suffix, ahead, behind):
    rows, width, _ = factors.shape
    count = source.shape[1]

    def turn(i, _):
        turned = factors[i].T
        high[i], low[i] = split(turned)
        return 0

    lax.fori_loop(0, rows, turn, 0)
    eye = (
        lax.broadcasted_iota(jnp.int32, (width, width), 0)
        == lax.broadcasted_iota(jnp.int32, (width, width), 1)
    ).astype(jnp.float32)
    ahead[:count] = jnp.zeros((count, width), jnp.float32)
    ahead[count:] = eye
    behind[...] = eye

    def step(i, _):
        j = rows - 1 - i
        moved = apply_split(ahead[...], high[i], low[i])
        back = apply_split(behind[...], high[j], low[j])
        state = moved[:count] + source[i]
        forward[i] = state
        prefix[i] = moved[count:]
        ahead[:count] = state
        ahead[count:] = moved[count:]
        suffix[j] = back
        behind[...] = back
        return 0

    lax.fori_loop(0, rows, step, 0)


def prepare(factors, source):
    rows, width, _ = factors.shape
    count = source.shape[1]
    square = (rows, width, width)
    return call(
        prepare_body,
        [
            shape(*square, dtype=jnp.bfloat16),
            shape(*square, dtype=jnp.bfloat16),
            shape(*source.shape),
            shape(*square),
            shape(*square),
        ],
        [pltpu.VMEM((count + width, width), jnp.float32), pltpu.VMEM((width, width), jnp.float32)],
        rows * 6 * (count + 2 * width) * width * width,
        factors,
        source,
    )


def couple_body(high, low, forward, prefix, suffix, first_end, cross, turn, twist, behind, ahead, kept):
    rows, count, width = forward.shape
    ahead[...] = jnp.zeros_like(ahead)
    behind[...] = jnp.zeros_like(behind)

    def step(i, _):
        j = rows - 1 - i
        entering = jnp.concatenate([forward[j], prefix[j]], axis=0) + behind[...]
        behind[...] = apply_split(entering, high[j], low[j])
        state = apply_split(ahead[...], high[i], low[i]) + suffix[i]
        ahead[...] = state
        kept[i] = state
        return 0

    lax.fori_loop(0, rows, step, 0)
    first_end[...] = behind[:count]
    cross[...] = behind[count:]
    turn[...] = ahead[...]
    ahead[...] = jnp.zeros_like(ahead)

    def back(i, _):
        j = rows - 1 - i
        ahead[...] = apply_split(kept[j] + ahead[...], high[j], low[j])
        return 0

    lax.fori_loop(0, rows, back, 0)
    twist[...] = ahead[...]


def couple(high, low, forward, prefix, suffix):
    rows, count, width = forward.shape
    square = (width, width)
    return call(
        couple_body,
        [shape(count, width), shape(*square), shape(*square), shape(*square)],
        [
            pltpu.VMEM((count + width, width), jnp.float32),
            pltpu.VMEM(square, jnp.float32),
            pltpu.VMEM((rows, *square), jnp.float32),
        ],
        rows * 6 * (count + 3 * width) * width * width,
        high,
        low,
        forward,
        prefix,
        suffix,
    )


def sweep_body(reverse, high, low, source, entering, result):
    rows = source.shape[0]

    def step(i, state):
        if reverse:
            j = rows - 1 - i
            state = apply_split(source[j] + state, high[j], low[j])
        else:
            j = i
            state = apply_split(state, high[j], low[j]) + source[j]
        result[j] = state
        return state

    lax.fori_loop(0, rows, step, entering[...], unroll=2)


def sweep(high, low, source, entering, reverse, after=None):
    rows, count, width = source.shape
    return call(
        functools.partial(sweep_body, reverse),
        [shape(*source.shape)],
        [],
        rows * 6 * count * width * width,
        high,
        low,
        source,
        entering,
        after=after,
    )[0]


def exchange(value, level):
    size = lax.axis_size(CHAIN)
    return lax.ppermute(value, CHAIN, [(i, i ^ (1 << level)) for i in range(size)])


def scan_spans(operator, total, reverse):
    width = operator.shape[0]
    count = total.shape[0]
    levels = (lax.axis_size(CHAIN) - 1).bit_length()
    span = jnp.concatenate([operator, total], axis=0)
    lead = None
    entering = jnp.zeros_like(total)
    arrivals = []
    for level in range(levels):
        after = (lax.axis_index(CHAIN) >> level) & 1 == (0 if reverse else 1)
        if level + 1 == levels:
            received = exchange(span[width:], level)
            return jnp.where(after, entering + matmul(received, lead), entering), arrivals
        received = exchange(span, level)
        first = jnp.where(after, received, span)
        second = jnp.where(after, span, received)
        source = jnp.concatenate([jnp.zeros_like(operator), second[width:]], axis=0)
        span = matmul(first, second[:width]) + source
        carried = received if lead is None else matmul(received, lead)
        base = jnp.eye(width, dtype=jnp.float32) if lead is None else lead
        lead = jnp.where(after, carried[:width], base)
        entering = jnp.where(after, entering + carried[width:], entering)
        arrivals.append(entering)


def join_body(position, spans, own, whole, reach, crossing):
    members, _, width, _ = spans.shape
    eye = (
        lax.broadcasted_iota(jnp.int32, (width, width), 0)
        == lax.broadcasted_iota(jnp.int32, (width, width), 1)
    ).astype(jnp.float32)
    reach[0] = eye
    reach[1] = eye
    mine = position[0]

    def outward(e, _):
        @pl.when(e == mine)
        def _():
            own[0] = reach[0]

        back = members - 1 - e

        @pl.when(back == mine)
        def _():
            own[1] = reach[1]

        ahead = reach[0]
        crossing[e] = apply_split(ahead, *split(spans[e, 2]))
        reach[1] = apply_split(reach[1], *split(spans[back, 1]))
        reach[0] = apply_split(ahead, *split(spans[e, 0]))
        return 0

    lax.fori_loop(0, members, outward, 0)
    whole[0] = reach[0]
    whole[1] = reach[1]
    reach[0] = jnp.zeros((width, width), jnp.float32)

    def inward(i, _):
        e = members - 1 - i

        @pl.when(e == mine)
        def _():
            own[2] = reach[0]

        reach[0] = apply_split(reach[0], *split(spans[e, 1])) + crossing[e]
        return 0

    lax.fori_loop(0, members, inward, 0)
    whole[2] = reach[0]


def join(position, spans, after):
    members, parts, width, _ = spans.shape
    return call(
        join_body,
        [shape(parts, width, width), shape(parts, width, width)],
        [pltpu.VMEM((2, width, width), jnp.float32), pltpu.VMEM((members, width, width), jnp.float32)],
        members * 6 * 4 * width**3,
        spans,
        after=after,
        position=position,
    )


def relay(mine, spans, ends, entered):
    members, _, width, _ = spans.shape
    count = (ends.shape[1] - 8) // 2
    state = jnp.zeros((count, width), jnp.float32)
    states = []
    for e in range(members):
        states.append(state)

        @pl.when(mine == e)
        def _(state=state):
            entered[0] = state

        end = ends[e, :count]
        state = end if e == 0 else apply_split(state, *split(spans[e, 0])) + end
    ahead = state
    state = jnp.zeros((count, width), jnp.float32)
    for e in reversed(range(members)):

        @pl.when(mine == e)
        def _(state=state):
            entered[1] = state

        end = ends[e, count : 2 * count]
        if e > 0:
            end = end + apply_split(states[e], *split(spans[e, 2]))
        state = end if e == members - 1 else apply_split(state, *split(spans[e, 1])) + end
    return ahead, state


def total_of(ends):
    count = (ends.shape[1] - 8) // 2
    total = ends[0, 2 * count :]
    for e in range(1, ends.shape[0]):
        total = total + ends[e, 2 * count :]
    return total


def near_body(position, spans, ends, entered, whole):
    count = entered.shape[1]
    ahead, behind = relay(position[0], spans, ends, entered)
    whole[:count] = ahead
    whole[count : 2 * count] = behind
    whole[2 * count :] = total_of(ends)


def near(position, spans, ends):
    members, length, width = ends.shape
    count = (length - 8) // 2
    return call(
        near_body,
        [shape(2, count, width), shape(length, width)],
        [],
        members * 6 * 3 * count * width * width,
        spans,
        ends,
        position=position,
    )


def far_body(position, spans, ends, own, inner, entering, squares, entered):
    relay(position[0], spans, ends, entered)
    ahead, behind = entered[0], entered[1]
    entering[0] = apply_split(ahead, *split(own[0])) + inner[0]
    entering[1] = (
        apply_split(behind, *split(own[1])) + apply_split(ahead, *split(own[2])) + inner[1]
    )
    squares[...] = total_of(ends)


def far(position, spans, ends, own, inner):
    members, length, width = ends.shape
    count = (length - 8) // 2
    return call(
        far_body,
        [shape(2, count, width), shape(8, width)],
        [pltpu.VMEM((2, count, width), jnp.float32)],
        members * 6 * 3 * count * width * width,
        spans,
        ends,
        own,
        inner,
        position=position,
    )


def row_sums(total):
    ones = jnp.ones((8, total.shape[1]), jnp.float32)
    return lax.dot_general(
        ones,
        total,
        (((1,), (1,)), ((), ())),
        precision=lax.Precision.HIGHEST,
        preferred_element_type=jnp.float32,
    )


def first_body(high, low, forward, entering, middle_ends, turn, twist, solved, message):
    rows, count, width = forward.shape

    def step(i, carry):
        state, total = carry
        j = rows - 1 - i
        state = apply_split(forward[j] + state, high[j], low[j])
        solved[j] = state
        return state, total + state * state

    start = entering[...]
    zero = jnp.zeros((count, width), jnp.float32)
    _, total = lax.fori_loop(0, rows, step, (start, zero), unroll=2)
    message[:count] = middle_ends[0] + apply_split(start, *split(turn[...]))
    message[count : 2 * count] = middle_ends[1] + apply_split(start, *split(twist[...]))
    message[2 * count :] = jnp.zeros((8, width), jnp.float32)
    message[2 * count :, :count] = row_sums(total)


def first_rows(high, low, forward, entering, middle_ends, turn, twist):
    rows, count, width = forward.shape
    return call(
        first_body,
        [shape(*forward.shape), shape(2 * count + 8, width)],
        [],
        rows * 6 * count * width * width,
        high,
        low,
        forward,
        entering,
        middle_ends,
        turn,
        twist,
    )


def second_body(high, low, source, entering, scale, result, squares, forward):
    rows, count, width = source.shape
    inverse = 1.0 / scale[...]

    def ahead(i, state):
        state = apply_split(state, high[i], low[i]) + source[i]
        forward[i] = state
        return state

    lax.fori_loop(0, rows, ahead, entering[0], unroll=2)

    def behind(i, carry):
        state, total = carry
        j = rows - 1 - i
        state = apply_split(forward[j] + state, high[j], low[j])
        value = state * inverse
        result[j] = value
        return state, total + value * value

    zero = jnp.zeros((count, width), jnp.float32)
    _, total = lax.fori_loop(0, rows, behind, (entering[1], zero), unroll=2)
    squares[...] = jnp.zeros(squares.shape, jnp.float32)
    squares[:, :count] = row_sums(total)


def second_rows(high, low, source, entering, scale):
    rows, count, width = source.shape
    return call(
        second_body,
        [shape(*source.shape), shape(8, 128)],
        [pltpu.VMEM(source.shape, jnp.float32)],
        2 * rows * 6 * count * width * width,
        high,
        low,
        source,
        entering,
        scale,
    )


def scale_body(vectors, scale, result):
    result[...] = vectors[...] * (1.0 / scale[...])[None]


def rescale(vectors, scale):
    return call(scale_body, [shape(*vectors.shape)], [], vectors.size, vectors, scale)[0]


def to_all(value, axis):
    copies = jnp.broadcast_to(value[None], (lax.axis_size(axis), *value.shape))
    return lax.all_to_all(copies, axis, 0, 0, tiled=True)


def shards(start_vectors, factors):
    rows, count, width = start_vectors.shape
    cell_count = rows * lax.axis_size(CHAIN) * width
    whole = lax.all_gather(factors, "cols", axis=1, tiled=True)
    high, low, forward, prefix, suffix = prepare(whole, start_vectors)
    first_end, cross, turn, twist = couple(high, low, forward, prefix, suffix)
    operators = jnp.stack([prefix[rows - 1], suffix[0], cross])
    near_spans = lax.all_gather(operators, "inner")
    near_position = lax.axis_index("inner").astype(jnp.int32)[None]
    far_position = lax.axis_index("outer").astype(jnp.int32)[None]
    zero = jnp.zeros((count, width), jnp.float32)

    entering, early = scan_spans(prefix[rows - 1], forward[rows - 1], False)
    end = first_end + matmul(entering, cross)
    own, composed = join(near_position, near_spans, early[-1])
    far_spans = lax.all_gather(composed, "outer")
    leaving, arrivals = scan_spans(suffix[0], end, True)
    forward = sweep(high, low, start_vectors, entering, False, arrivals[0])
    middle = sweep(high, low, forward, zero, True, arrivals[1])
    middle = sweep(high, low, middle, zero, False, arrivals[2])
    middle_ahead = middle[rows - 1]
    middle_behind = sweep(high, low, middle, zero, True, arrivals[-2])[0]
    entering = leaving

    middle_ends = jnp.stack([middle_ahead, middle_behind])
    first_solve, message = first_rows(high, low, forward, entering, middle_ends, turn, twist)
    inner, message = near(near_position, near_spans, to_all(message, "inner"))
    entering, squares = far(far_position, far_spans, to_all(message, "outer"), own, inner)
    scale_one = jnp.sqrt(squares[0, :count] / cell_count + eps_value)
    second, squares = second_rows(high, low, first_solve, entering, scale_one[:, None])
    squares = jnp.sum(to_all(squares, "inner"), axis=0)
    squares = jnp.sum(to_all(squares, "outer"), axis=0)
    scale_two = jnp.sqrt(squares[0, :count] / cell_count + eps_value)
    return rescale(second, scale_two[:, None]), jnp.log(scale_two)


def solution(mesh):
    size = mesh.shape["chain"]
    inner = 1 << ((size - 1).bit_length() // 2)
    devices = mesh.devices.reshape(size // inner, inner, mesh.shape["cols"])
    placed = P(CHAIN, "cols", None)
    return jax.shard_map(
        shards,
        mesh=Mesh(devices, (*CHAIN, "cols")),
        in_specs=(placed, placed),
        out_specs=(placed, P("cols")),
        check_vma=False,
    )
```

```python
import functools

import jax
import jax.numpy as jnp
from jax import lax
from jax.experimental import pallas as pl
from jax.experimental.pallas import tpu as pltpu
from jax.sharding import Mesh, PartitionSpec as P

eps_value = 1e-06
VMEM_BYTES = 56 * 1024 * 1024
CHAIN = ("outer", "inner")


def split(value):
    high = value.astype(jnp.bfloat16)
    low = (value - high.astype(jnp.float32)).astype(jnp.bfloat16)
    return high, low


def apply_split(state, high, low):
    rows = state.shape[0]
    state_high, state_low = split(state)
    both = jnp.dot(
        jnp.concatenate([state_high, state_low], axis=0),
        high,
        preferred_element_type=jnp.float32,
    )
    return (both[:rows] + both[rows:]) + jnp.dot(
        state_high, low, preferred_element_type=jnp.float32
    )


def call(body, out_shapes, scratch, flops, *operands, after=(), position=None):
    vmem = pl.BlockSpec(memory_space=pltpu.VMEM)
    touched = sum(x.size * x.dtype.itemsize for x in (*operands, *out_shapes))
    specs = [vmem] * len(operands)
    if position is not None:
        specs = [pl.BlockSpec(memory_space=pltpu.SMEM), *specs]
        operands = (position, *operands)
    kernel = body
    if after:
        specs = [pl.BlockSpec(memory_space=pl.ANY)] * len(after) + specs
        operands = (*after, *operands)

        def kernel(*refs):
            body(*refs[len(after) :])

    return pl.pallas_call(
        kernel,
        out_shape=tuple(out_shapes),
        in_specs=specs,
        out_specs=tuple([vmem] * len(out_shapes)),
        scratch_shapes=scratch,
        compiler_params=pltpu.CompilerParams(vmem_limit_bytes=VMEM_BYTES),
        cost_estimate=pl.CostEstimate(flops=flops, bytes_accessed=touched, transcendentals=0),
    )(*operands)


def shape(*dims, dtype=jnp.float32):
    return jax.ShapeDtypeStruct(dims, dtype)


def prepare_body(factors, source, high, low, suffix, cross, solved, operators, ends, prefix, forward, ahead, behind):
    rows, width, _ = factors.shape
    count = source.shape[1]

    def turn(i, _):
        high[i], low[i] = split(factors[i].T)
        return 0

    lax.fori_loop(0, rows, turn, 0)
    eye = identity(width)
    ahead[:count] = jnp.zeros((count, width), jnp.float32)
    ahead[count:] = eye
    behind[...] = eye

    def step(i, _):
        j = rows - 1 - i
        moved = apply_split(ahead[...], high[i], low[i])
        back = apply_split(behind[...], high[j], low[j])
        state = moved[:count] + source[i]
        forward[i] = state
        prefix[i] = moved[count:]
        ahead[:count] = state
        ahead[count:] = moved[count:]
        suffix[j] = back
        behind[...] = back
        return 0

    lax.fori_loop(0, rows, step, 0)
    operators[0] = ahead[count:]
    operators[1] = behind[...]
    ends[:count] = ahead[:count]
    ahead[...] = jnp.zeros_like(ahead)

    def back(i, _):
        j = rows - 1 - i
        entering = jnp.concatenate([forward[j], prefix[j]], axis=0) + ahead[...]
        state = apply_split(entering, high[j], low[j])
        ahead[...] = state
        solved[j] = state[:count]
        cross[j] = state[count:]
        return 0

    lax.fori_loop(0, rows, back, 0)
    operators[2] = ahead[count:]
    ends[count : 2 * count] = ahead[:count]
    ends[2 * count :] = jnp.zeros((8, width), jnp.float32)


def prepare(factors, source):
    rows, width, _ = factors.shape
    count = source.shape[1]
    square = (rows, width, width)
    return call(
        prepare_body,
        [
            shape(*square, dtype=jnp.bfloat16),
            shape(*square, dtype=jnp.bfloat16),
            shape(*square),
            shape(*square),
            shape(*source.shape),
            shape(3, width, width),
            shape(2 * count + 8, width),
        ],
        [
            pltpu.VMEM(square, jnp.float32),
            pltpu.VMEM(source.shape, jnp.float32),
            pltpu.VMEM((count + width, width), jnp.float32),
            pltpu.VMEM((width, width), jnp.float32),
        ],
        rows * 6 * (2 * count + 3 * width) * width * width,
        factors,
        source,
    )


def ahead_body(high, low, cross, suffix, solved, rows_out, ends):
    rows, count, width = solved.shape
    ends[...] = jnp.zeros_like(ends)

    def step(i, _):
        source = jnp.concatenate([cross[i], suffix[i], solved[i]], axis=0)
        state = apply_split(ends[...], high[i], low[i]) + source
        ends[...] = state
        rows_out[i] = state
        return 0

    lax.fori_loop(0, rows, step, 0)


def behind_body(high, low, source, ends):
    rows = source.shape[0]
    ends[...] = jnp.zeros_like(ends)

    def step(i, _):
        j = rows - 1 - i
        ends[...] = apply_split(source[j] + ends[...], high[j], low[j])
        return 0

    lax.fori_loop(0, rows, step, 0)


def respond_ahead(high, low, cross, suffix, solved):
    rows, count, width = solved.shape
    length = 2 * width + count
    return call(
        ahead_body,
        [shape(rows, length, width), shape(length, width)],
        [],
        rows * 6 * length * width * width,
        high,
        low,
        cross,
        suffix,
        solved,
    )


def respond_behind(high, low, source, after):
    rows, length, width = source.shape
    return call(
        behind_body,
        [shape(length, width)],
        [],
        rows * 6 * length * width * width,
        high,
        low,
        source,
        after=after,
    )[0]


def identity(width):
    return (
        lax.broadcasted_iota(jnp.int32, (width, width), 0)
        == lax.broadcasted_iota(jnp.int32, (width, width), 1)
    ).astype(jnp.float32)


def join_body(position, spans, own, whole, reach, crossing):
    members, _, width, _ = spans.shape
    eye = identity(width)
    reach[0] = eye
    reach[1] = eye
    mine = position[0]

    def outward(e, _):
        @pl.when(e == mine)
        def _():
            own[0] = reach[0]

        back = members - 1 - e

        @pl.when(back == mine)
        def _():
            own[1] = reach[1]

        ahead = reach[0]
        crossing[e] = apply_split(ahead, *split(spans[e, 2]))
        reach[1] = apply_split(reach[1], *split(spans[back, 1]))
        reach[0] = apply_split(ahead, *split(spans[e, 0]))
        return 0

    lax.fori_loop(0, members, outward, 0)
    whole[0] = reach[0]
    whole[1] = reach[1]
    reach[0] = jnp.zeros((width, width), jnp.float32)

    def inward(i, _):
        e = members - 1 - i

        @pl.when(e == mine)
        def _():
            own[2] = reach[0]

        reach[0] = apply_split(reach[0], *split(spans[e, 1])) + crossing[e]
        return 0

    lax.fori_loop(0, members, inward, 0)
    whole[2] = reach[0]


def join(position, spans, after):
    members, parts, width, _ = spans.shape
    return call(
        join_body,
        [shape(parts, width, width), shape(parts, width, width)],
        [pltpu.VMEM((2, width, width), jnp.float32), pltpu.VMEM((members, width, width), jnp.float32)],
        members * 6 * 4 * width**3,
        spans,
        after=after,
        position=position,
    )


def relay(mine, spans, ends, entered):
    members, _, width, _ = spans.shape
    count = (ends.shape[1] - 8) // 2
    state = jnp.zeros((count, width), jnp.float32)
    states = []
    for e in range(members):
        states.append(state)

        @pl.when(mine == e)
        def _(state=state):
            entered[0] = state

        end = ends[e, :count]
        state = end if e == 0 else apply_split(state, *split(spans[e, 0])) + end
    ahead = state
    state = jnp.zeros((count, width), jnp.float32)
    for e in reversed(range(members)):

        @pl.when(mine == e)
        def _(state=state):
            entered[1] = state

        end = ends[e, count : 2 * count]
        if e > 0:
            end = end + apply_split(states[e], *split(spans[e, 2]))
        state = end if e == members - 1 else apply_split(state, *split(spans[e, 1])) + end
    return ahead, state


def total_of(ends):
    count = (ends.shape[1] - 8) // 2
    total = ends[0, 2 * count :]
    for e in range(1, ends.shape[0]):
        total = total + ends[e, 2 * count :]
    return total


def near_body(position, spans, ends, entered, whole):
    count = entered.shape[1]
    ahead, behind = relay(position[0], spans, ends, entered)
    whole[:count] = ahead
    whole[count : 2 * count] = behind
    whole[2 * count :] = total_of(ends)


def near(position, spans, ends):
    members, length, width = ends.shape
    count = (length - 8) // 2
    return call(
        near_body,
        [shape(2, count, width), shape(length, width)],
        [],
        members * 6 * 3 * count * width * width,
        spans,
        ends,
        position=position,
    )


def far_body(position, spans, ends, own, inner, entering, squares, entered):
    relay(position[0], spans, ends, entered)
    ahead, behind = entered[0], entered[1]
    entering[0] = apply_split(ahead, *split(own[0])) + inner[0]
    entering[1] = (
        apply_split(behind, *split(own[1])) + apply_split(ahead, *split(own[2])) + inner[1]
    )
    squares[...] = total_of(ends)


def far(position, spans, ends, own, inner):
    members, length, width = ends.shape
    count = (length - 8) // 2
    return call(
        far_body,
        [shape(2, count, width), shape(8, width)],
        [pltpu.VMEM((2, count, width), jnp.float32)],
        members * 6 * 3 * count * width * width,
        spans,
        ends,
        own,
        inner,
        position=position,
    )


def row_sums(total):
    ones = jnp.ones((8, total.shape[1]), jnp.float32)
    return lax.dot_general(
        ones,
        total,
        (((1,), (1,)), ((), ())),
        precision=lax.Precision.HIGHEST,
        preferred_element_type=jnp.float32,
    )


def first_body(high, low, source, entering, ahead_ends, behind_ends, solved, message, forward):
    rows, count, width = source.shape

    def ahead(i, state):
        state = apply_split(state, high[i], low[i]) + source[i]
        forward[i] = state
        return state

    lax.fori_loop(0, rows, ahead, entering[0], unroll=2)

    def behind(i, carry):
        state, total = carry
        j = rows - 1 - i
        state = apply_split(forward[j] + state, high[j], low[j])
        solved[j] = state
        return state, total + state * state

    zero = jnp.zeros((count, width), jnp.float32)
    _, total = lax.fori_loop(0, rows, behind, (entering[1], zero), unroll=2)
    for place, ends in enumerate((ahead_ends, behind_ends)):
        message[place * count : (place + 1) * count] = (
            ends[2 * width :]
            + apply_split(entering[0], *split(ends[:width]))
            + apply_split(entering[1], *split(ends[width : 2 * width]))
        )
    message[2 * count :] = jnp.zeros((8, width), jnp.float32)
    message[2 * count :, :count] = row_sums(total)


def first_rows(high, low, source, entering, ahead_ends, behind_ends):
    rows, count, width = source.shape
    return call(
        first_body,
        [shape(*source.shape), shape(2 * count + 8, width)],
        [pltpu.VMEM(source.shape, jnp.float32)],
        2 * rows * 6 * count * width * width,
        high,
        low,
        source,
        entering,
        ahead_ends,
        behind_ends,
    )


def second_body(high, low, source, entering, scale, result, squares, forward):
    rows, count, width = source.shape
    inverse = 1.0 / scale[...]

    def ahead(i, state):
        state = apply_split(state, high[i], low[i]) + source[i]
        forward[i] = state
        return state

    lax.fori_loop(0, rows, ahead, entering[0], unroll=2)

    def behind(i, carry):
        state, total = carry
        j = rows - 1 - i
        state = apply_split(forward[j] + state, high[j], low[j])
        value = state * inverse
        result[j] = value
        return state, total + value * value

    zero = jnp.zeros((count, width), jnp.float32)
    _, total = lax.fori_loop(0, rows, behind, (entering[1], zero), unroll=2)
    squares[...] = jnp.zeros(squares.shape, jnp.float32)
    squares[:, :count] = row_sums(total)


def second_rows(high, low, source, entering, scale):
    rows, count, width = source.shape
    return call(
        second_body,
        [shape(*source.shape), shape(8, 128)],
        [pltpu.VMEM(source.shape, jnp.float32)],
        2 * rows * 6 * count * width * width,
        high,
        low,
        source,
        entering,
        scale,
    )


def scale_body(vectors, scale, result):
    result[...] = vectors[...] * (1.0 / scale[...])[None]


def rescale(vectors, scale):
    return call(scale_body, [shape(*vectors.shape)], [], vectors.size, vectors, scale)[0]


def to_all(value, axis):
    copies = jnp.broadcast_to(value[None], (lax.axis_size(axis), *value.shape))
    return lax.all_to_all(copies, axis, 0, 0, tiled=True)


def shards(start_vectors, factors):
    rows, count, width = start_vectors.shape
    cell_count = rows * lax.axis_size(CHAIN) * width
    whole = lax.all_gather(factors, "cols", axis=1, tiled=True)
    high, low, suffix, cross, solved, operators, ends = prepare(whole, start_vectors)
    near_position = lax.axis_index("inner").astype(jnp.int32)[None]
    far_position = lax.axis_index("outer").astype(jnp.int32)[None]
    near_spans = lax.all_gather(operators, "inner")
    near_ends = to_all(ends, "inner")
    ahead_rows, ahead_ends = respond_ahead(high, low, cross, suffix, solved)
    own, composed = join(near_position, near_spans, (ahead_ends, near_ends))
    far_spans = lax.all_gather(composed, "outer")
    behind_ends = respond_behind(high, low, ahead_rows, (own,))

    inner, message = near(near_position, near_spans, near_ends)
    entering, _ = far(far_position, far_spans, to_all(message, "outer"), own, inner)
    first_solve, message = first_rows(
        high, low, start_vectors, entering, ahead_ends, behind_ends
    )
    inner, message = near(near_position, near_spans, to_all(message, "inner"))
    entering, squares = far(far_position, far_spans, to_all(message, "outer"), own, inner)
    scale_one = jnp.sqrt(squares[0, :count] / cell_count + eps_value)
    second, squares = second_rows(high, low, first_solve, entering, scale_one[:, None])
    squares = jnp.sum(to_all(squares, "inner"), axis=0)
    squares = jnp.sum(to_all(squares, "outer"), axis=0)
    scale_two = jnp.sqrt(squares[0, :count] / cell_count + eps_value)
    return rescale(second, scale_two[:, None]), jnp.log(scale_two)


def solution(mesh):
    size = mesh.shape["chain"]
    inner = 1 << ((size - 1).bit_length() // 2)
    devices = mesh.devices.reshape(size // inner, inner, mesh.shape["cols"])
    placed = P(CHAIN, "cols", None)
    return jax.shard_map(
        shards,
        mesh=Mesh(devices, (*CHAIN, "cols")),
        in_specs=(placed, placed),
        out_specs=(placed, P("cols")),
        check_vma=False,
    )
```

```python
import functools

import jax
import jax.numpy as jnp
from jax import lax
from jax.experimental import pallas as pl
from jax.experimental.pallas import tpu as pltpu
from jax.sharding import Mesh, PartitionSpec as P

eps_value = 1e-06
VMEM_BYTES = 56 * 1024 * 1024
INNER = ("mid", "core")
CHAIN = ("outer", *INNER)


def split(value):
    high = value.astype(jnp.bfloat16)
    low = (value - high.astype(jnp.float32)).astype(jnp.bfloat16)
    return high, low


def apply_split(state, high, low):
    rows = state.shape[0]
    state_high, state_low = split(state)
    both = jnp.dot(
        jnp.concatenate([state_high, state_low], axis=0),
        high,
        preferred_element_type=jnp.float32,
    )
    return (both[:rows] + both[rows:]) + jnp.dot(
        state_high, low, preferred_element_type=jnp.float32
    )


def call(body, out_shapes, scratch, flops, *operands, after=(), position=None):
    vmem = pl.BlockSpec(memory_space=pltpu.VMEM)
    touched = sum(x.size * x.dtype.itemsize for x in (*operands, *out_shapes))
    specs = [vmem] * len(operands)
    if position is not None:
        specs = [pl.BlockSpec(memory_space=pltpu.SMEM), *specs]
        operands = (position, *operands)
    kernel = body
    if after:
        specs = [pl.BlockSpec(memory_space=pl.ANY)] * len(after) + specs
        operands = (*after, *operands)

        def kernel(*refs):
            body(*refs[len(after) :])

    return pl.pallas_call(
        kernel,
        out_shape=tuple(out_shapes),
        in_specs=specs,
        out_specs=tuple([vmem] * len(out_shapes)),
        scratch_shapes=scratch,
        compiler_params=pltpu.CompilerParams(vmem_limit_bytes=VMEM_BYTES),
        cost_estimate=pl.CostEstimate(flops=flops, bytes_accessed=touched, transcendentals=0),
    )(*operands)


def gate(value, after):
    anywhere = pl.BlockSpec(memory_space=pl.ANY)
    return pl.pallas_call(
        lambda *refs: None,
        out_shape=shape(*value.shape, dtype=value.dtype),
        in_specs=[anywhere] * (1 + len(after)),
        out_specs=anywhere,
        input_output_aliases={0: 0},
    )(value, *after)


def shape(*dims, dtype=jnp.float32):
    return jax.ShapeDtypeStruct(dims, dtype)


def prepare_body(factors, source, high, low, suffix, cross, solved, operators, ends, prefix, forward, ahead, behind):
    rows, width, _ = factors.shape
    count = source.shape[1]

    def turn(i, _):
        high[i], low[i] = split(factors[i].T)
        return 0

    lax.fori_loop(0, rows, turn, 0)
    eye = identity(width)
    ahead[:count] = jnp.zeros((count, width), jnp.float32)
    ahead[count:] = eye
    behind[...] = eye

    def step(i, _):
        j = rows - 1 - i
        moved = apply_split(ahead[...], high[i], low[i])
        back = apply_split(behind[...], high[j], low[j])
        state = moved[:count] + source[i]
        forward[i] = state
        prefix[i] = moved[count:]
        ahead[:count] = state
        ahead[count:] = moved[count:]
        suffix[j] = back
        behind[...] = back
        return 0

    lax.fori_loop(0, rows, step, 0)
    operators[0] = ahead[count:]
    operators[1] = behind[...]
    ahead[...] = jnp.zeros_like(ahead)

    def back(i, _):
        j = rows - 1 - i
        entering = jnp.concatenate([forward[j], prefix[j]], axis=0) + ahead[...]
        state = apply_split(entering, high[j], low[j])
        ahead[...] = state
        solved[j] = state[:count]
        cross[j] = state[count:]
        return 0

    lax.fori_loop(0, rows, back, 0)
    operators[2] = ahead[count:]
    for member in range(ends.shape[0]):
        ends[member, :count] = forward[rows - 1]
        ends[member, count : 2 * count] = ahead[:count]
        ends[member, 2 * count :] = jnp.zeros((8, width), jnp.float32)


def prepare(factors, source, copies):
    rows, width, _ = factors.shape
    count = source.shape[1]
    square = (rows, width, width)
    return call(
        prepare_body,
        [
            shape(*square, dtype=jnp.bfloat16),
            shape(*square, dtype=jnp.bfloat16),
            shape(*square),
            shape(*square),
            shape(*source.shape),
            shape(3, width, width),
            shape(copies, 2 * count + 8, width),
        ],
        [
            pltpu.VMEM(square, jnp.float32),
            pltpu.VMEM(source.shape, jnp.float32),
            pltpu.VMEM((count + width, width), jnp.float32),
            pltpu.VMEM((width, width), jnp.float32),
        ],
        rows * 6 * (2 * count + 3 * width) * width * width,
        factors,
        source,
    )


def ahead_body(high, low, cross, suffix, solved, rows_out, ends):
    rows, count, width = solved.shape
    ends[...] = jnp.zeros_like(ends)

    def step(i, _):
        source = jnp.concatenate([cross[i], suffix[i], solved[i]], axis=0)
        state = apply_split(ends[...], high[i], low[i]) + source
        ends[...] = state
        rows_out[i] = state
        return 0

    lax.fori_loop(0, rows, step, 0)


def behind_body(high, low, source, ends):
    rows = source.shape[0]
    ends[...] = jnp.zeros_like(ends)

    def step(i, _):
        j = rows - 1 - i
        ends[...] = apply_split(source[j] + ends[...], high[j], low[j])
        return 0

    lax.fori_loop(0, rows, step, 0)


def respond_ahead(high, low, cross, suffix, solved):
    rows, count, width = solved.shape
    length = 2 * width + count
    return call(
        ahead_body,
        [shape(rows, length, width), shape(length, width)],
        [],
        rows * 6 * length * width * width,
        high,
        low,
        cross,
        suffix,
        solved,
    )


def respond_behind(high, low, source, after):
    rows, length, width = source.shape
    return call(
        behind_body,
        [shape(length, width)],
        [],
        rows * 6 * length * width * width,
        high,
        low,
        source,
        after=after,
    )[0]


def identity(width):
    return (
        lax.broadcasted_iota(jnp.int32, (width, width), 0)
        == lax.broadcasted_iota(jnp.int32, (width, width), 1)
    ).astype(jnp.float32)


def row_span(place, own, other, e, part):
    return jnp.where(e % 2 == place[1], own[e // 2, part], other[e // 2, part])


def far_span(place, own, other, e, part):
    first = place[1] == 0
    return jnp.concatenate(
        [
            jnp.where(first, own[e, part], other[e, part]),
            jnp.where(first, other[e, part], own[e, part]),
        ],
        axis=0,
    )


def join_body(place, spans, others, own, half, reach, crossing):
    members = 2 * spans.shape[0]
    width = spans.shape[2]
    reach[0] = identity(width)
    reach[1] = identity(width)
    mine = place[0]
    kept = pl.ds(pl.multiple_of(place[1] * (width // 2), width // 2), width // 2)

    def span(e, part):
        return split(row_span(place, spans, others, e, part))

    def outward(e, _):
        @pl.when(e == mine)
        def _():
            own[0] = reach[0]

        back = members - 1 - e

        @pl.when(back == mine)
        def _():
            own[1] = reach[1]

        ahead = reach[0]
        crossing[e] = apply_split(ahead, *span(e, 2))
        reach[1] = apply_split(reach[1], *span(back, 1))
        reach[0] = apply_split(ahead, *span(e, 0))
        return 0

    lax.fori_loop(0, members, outward, 0)
    half[0] = reach[0, kept]
    half[1] = reach[1, kept]
    reach[0] = jnp.zeros((width, width), jnp.float32)

    def inward(i, _):
        e = members - 1 - i

        @pl.when(e == mine)
        def _():
            own[2] = reach[0]

        reach[0] = apply_split(reach[0], *span(e, 1)) + crossing[e]
        return 0

    lax.fori_loop(0, members, inward, 0)
    half[2] = reach[0, kept]


def join(place, spans, others):
    chips, parts, width, _ = spans.shape
    return call(
        join_body,
        [shape(parts, width, width), shape(parts, width // 2, width)],
        [
            pltpu.VMEM((2, width, width), jnp.float32),
            pltpu.VMEM((2 * chips, width, width), jnp.float32),
        ],
        2 * chips * 6 * 4 * width**3,
        spans,
        others,
        position=place,
    )


def relay(span, ends, states):
    members, length, width = ends.shape
    count = (length - 8) // 2
    state = jnp.zeros((count, width), jnp.float32)
    entered = []
    for e in range(members):
        entered.append(state)
        states[0, e] = state
        end = ends[e, :count]
        state = end if e == 0 else apply_split(state, *split(span(e, 0))) + end
    ahead = state
    state = jnp.zeros((count, width), jnp.float32)
    for e in reversed(range(members)):
        states[1, e] = state
        end = ends[e, count : 2 * count]
        if e > 0:
            end = end + apply_split(entered[e], *split(span(e, 2)))
        state = end if e == members - 1 else apply_split(state, *split(span(e, 1))) + end
    return ahead, state


def total_of(ends):
    count = (ends.shape[1] - 8) // 2
    total = ends[0, 2 * count :]
    for e in range(1, ends.shape[0]):
        total = total + ends[e, 2 * count :]
    return total


def near_body(place, spans, others, ends, entered, messages, states):
    count = entered.shape[1]
    ahead, behind = relay(functools.partial(row_span, place, spans, others), ends, states)
    message = jnp.concatenate([ahead, behind, total_of(ends)], axis=0)
    for member in range(messages.shape[0]):
        messages[member] = message
    entered[0] = states[0, place[0]]
    entered[1] = states[1, place[0]]


def near(place, spans, others, ends, copies):
    members, length, width = ends.shape
    count = (length - 8) // 2
    return call(
        near_body,
        [shape(2, count, width), shape(copies, length, width)],
        [pltpu.VMEM((2, members, count, width), jnp.float32)],
        members * 6 * 3 * count * width * width,
        spans,
        others,
        ends,
        position=place,
    )


def far_body(place, spans, others, ends, own, inner, entering, squares, states):
    relay(functools.partial(far_span, place, spans, others), ends, states)
    ahead, behind = states[0, place[0]], states[1, place[0]]
    entering[0] = apply_split(ahead, *split(own[0])) + inner[0]
    entering[1] = (
        apply_split(behind, *split(own[1])) + apply_split(ahead, *split(own[2])) + inner[1]
    )
    squares[...] = total_of(ends)


def far(place, spans, others, ends, own, inner):
    members, length, width = ends.shape
    count = (length - 8) // 2
    return call(
        far_body,
        [shape(2, count, width), shape(8, width)],
        [pltpu.VMEM((2, members, count, width), jnp.float32)],
        members * 6 * 3 * count * width * width,
        spans,
        others,
        ends,
        own,
        inner,
        position=place,
    )


def row_sums(total):
    ones = jnp.ones((8, total.shape[1]), jnp.float32)
    return lax.dot_general(
        ones,
        total,
        (((1,), (1,)), ((), ())),
        precision=lax.Precision.HIGHEST,
        preferred_element_type=jnp.float32,
    )


def first_body(high, low, source, entering, ahead_ends, behind_ends, solved, messages, forward):
    rows, count, width = source.shape

    def ahead(i, state):
        state = apply_split(state, high[i], low[i]) + source[i]
        forward[i] = state
        return state

    lax.fori_loop(0, rows, ahead, entering[0], unroll=2)

    def behind(i, carry):
        state, total = carry
        j = rows - 1 - i
        state = apply_split(forward[j] + state, high[j], low[j])
        solved[j] = state
        return state, total + state * state

    zero = jnp.zeros((count, width), jnp.float32)
    _, total = lax.fori_loop(0, rows, behind, (entering[1], zero), unroll=2)
    parts = [
        ends[2 * width :]
        + apply_split(entering[0], *split(ends[:width]))
        + apply_split(entering[1], *split(ends[width : 2 * width]))
        for ends in (ahead_ends, behind_ends)
    ]
    sums = row_sums(total)
    for member in range(messages.shape[0]):
        messages[member, :count] = parts[0]
        messages[member, count : 2 * count] = parts[1]
        messages[member, 2 * count :] = jnp.zeros((8, width), jnp.float32)
        messages[member, 2 * count :, :count] = sums


def first_rows(high, low, source, entering, ahead_ends, behind_ends, copies):
    rows, count, width = source.shape
    return call(
        first_body,
        [shape(*source.shape), shape(copies, 2 * count + 8, width)],
        [pltpu.VMEM(source.shape, jnp.float32)],
        2 * rows * 6 * count * width * width,
        high,
        low,
        source,
        entering,
        ahead_ends,
        behind_ends,
    )


def second_body(high, low, source, entering, scale, result, squares, forward):
    rows, count, width = source.shape
    inverse = 1.0 / scale[...]

    def ahead(i, state):
        state = apply_split(state, high[i], low[i]) + source[i]
        forward[i] = state
        return state

    lax.fori_loop(0, rows, ahead, entering[0], unroll=2)

    def behind(i, carry):
        state, total = carry
        j = rows - 1 - i
        state = apply_split(forward[j] + state, high[j], low[j])
        value = state * inverse
        result[j] = value
        return state, total + value * value

    zero = jnp.zeros((count, width), jnp.float32)
    _, total = lax.fori_loop(0, rows, behind, (entering[1], zero), unroll=2)
    squares[...] = jnp.zeros(squares.shape, jnp.float32)
    sums = row_sums(total)
    for member in range(squares.shape[0]):
        squares[member, :, :count] = sums


def second_rows(high, low, source, entering, scale, copies):
    rows, count, width = source.shape
    return call(
        second_body,
        [shape(*source.shape), shape(copies, 8, 128)],
        [pltpu.VMEM(source.shape, jnp.float32)],
        2 * rows * 6 * count * width * width,
        high,
        low,
        source,
        entering,
        scale,
    )


def scale_body(vectors, scale, result):
    result[...] = vectors[...] * (1.0 / scale[...])[None]


def rescale(vectors, scale):
    return call(scale_body, [shape(*vectors.shape)], [], vectors.size, vectors, scale)[0]


def swap(value, axis):
    return lax.all_to_all(value, axis, 0, 0, tiled=True)


def shards(start_vectors, factors):
    rows, count, width = start_vectors.shape
    cell_count = rows * lax.axis_size(CHAIN) * width
    members, groups = lax.axis_size(INNER), lax.axis_size("outer")
    core = lax.axis_index("core")
    near_place = jnp.stack([lax.axis_index(INNER), core]).astype(jnp.int32)
    far_place = jnp.stack([lax.axis_index("outer"), core]).astype(jnp.int32)
    cross_core = functools.partial(lax.ppermute, axis_name="core", perm=[(0, 1), (1, 0)])

    whole = lax.all_gather(factors, "cols", axis=1, tiled=True)
    high, low, suffix, cross, solved, operators, ends = prepare(whole, start_vectors, members)
    own_spans = lax.all_gather(operators, "mid")
    near_ends = swap(ends, INNER)
    ahead_rows, ahead_ends = respond_ahead(high, low, cross, suffix, solved)
    own_spans = gate(own_spans, (near_ends, ahead_ends))
    near_spans = (own_spans, cross_core(own_spans))
    own, half = join(near_place, *near_spans)
    own_halves = lax.all_gather(half, "outer")
    behind_ends = respond_behind(high, low, ahead_rows, (own,))
    inner, message = near(near_place, *near_spans, near_ends, groups)
    far_ends = swap(message, "outer")
    own_halves = gate(own_halves, (far_ends, behind_ends))
    far_spans = (own_halves, cross_core(own_halves))
    entering, _ = far(far_place, *far_spans, far_ends, own, inner)

    first_solve, message = first_rows(
        high, low, start_vectors, entering, ahead_ends, behind_ends, members
    )
    inner, message = near(near_place, *near_spans, swap(message, INNER), groups)
    entering, squares = far(far_place, *far_spans, swap(message, "outer"), own, inner)
    scale_one = jnp.sqrt(squares[0, :count] / cell_count + eps_value)
    second, squares = second_rows(
        high, low, first_solve, entering, scale_one[:, None], members
    )
    squares = jnp.sum(swap(squares, INNER), axis=0)
    squares = jnp.broadcast_to(squares[None], (groups, *squares.shape))
    squares = jnp.sum(swap(squares, "outer"), axis=0)
    scale_two = jnp.sqrt(squares[0, :count] / cell_count + eps_value)
    return rescale(second, scale_two[:, None]), jnp.log(scale_two)


def solution(mesh):
    size = mesh.shape["chain"]
    outer = 1 << ((size - 1).bit_length() // 2)
    devices = mesh.devices.reshape(outer, size // outer // 2, 2, mesh.shape["cols"])
    placed = P(CHAIN, "cols", None)
    return jax.shard_map(
        shards,
        mesh=Mesh(devices, (*CHAIN, "cols")),
        in_specs=(placed, placed),
        out_specs=(placed, P("cols")),
        check_vma=False,
    )
```

```python
import functools

import jax
import jax.numpy as jnp
from jax import lax
from jax.experimental import pallas as pl
from jax.experimental.pallas import tpu as pltpu
from jax.sharding import Mesh, PartitionSpec as P

eps_value = 1e-06
VMEM_BYTES = 56 * 1024 * 1024
INNER = ("mid", "core")
CHAIN = ("outer", *INNER)


def split(value):
    high = value.astype(jnp.bfloat16)
    low = (value - high.astype(jnp.float32)).astype(jnp.bfloat16)
    return high, low


def apply_split(state, high, low):
    rows = state.shape[0]
    state_high, state_low = split(state)
    both = jnp.dot(
        jnp.concatenate([state_high, state_low], axis=0),
        high,
        preferred_element_type=jnp.float32,
    )
    return (both[:rows] + both[rows:]) + jnp.dot(
        state_high, low, preferred_element_type=jnp.float32
    )


def call(body, out_shapes, scratch, flops, *operands, after=(), position=None):
    vmem = pl.BlockSpec(memory_space=pltpu.VMEM)
    touched = sum(x.size * x.dtype.itemsize for x in (*operands, *out_shapes))
    specs = [vmem] * len(operands)
    if position is not None:
        specs = [pl.BlockSpec(memory_space=pltpu.SMEM), *specs]
        operands = (position, *operands)
    kernel = body
    if after:
        specs = [pl.BlockSpec(memory_space=pl.ANY)] * len(after) + specs
        operands = (*after, *operands)

        def kernel(*refs):
            body(*refs[len(after) :])

    return pl.pallas_call(
        kernel,
        out_shape=tuple(out_shapes),
        in_specs=specs,
        out_specs=tuple([vmem] * len(out_shapes)),
        scratch_shapes=scratch,
        compiler_params=pltpu.CompilerParams(vmem_limit_bytes=VMEM_BYTES),
        cost_estimate=pl.CostEstimate(flops=flops, bytes_accessed=touched, transcendentals=0),
    )(*operands)


def gate(value, after):
    anywhere = pl.BlockSpec(memory_space=pl.ANY)
    return pl.pallas_call(
        lambda *refs: None,
        out_shape=shape(*value.shape, dtype=value.dtype),
        in_specs=[anywhere] * (1 + len(after)),
        out_specs=anywhere,
        input_output_aliases={0: 0},
    )(value, *after)


def shape(*dims, dtype=jnp.float32):
    return jax.ShapeDtypeStruct(dims, dtype)


def prepare_body(factors, source, high, low, suffix, cross, solved, operators, ends, prefix, forward, ahead, behind):
    rows, width, _ = factors.shape
    count = source.shape[1]

    def turn(i, _):
        high[i], low[i] = split(factors[i].T)
        return 0

    lax.fori_loop(0, rows, turn, 0)
    eye = identity(width)
    ahead[:count] = jnp.zeros((count, width), jnp.float32)
    ahead[count:] = eye
    behind[...] = eye

    def step(i, _):
        j = rows - 1 - i
        moved = apply_split(ahead[...], high[i], low[i])
        back = apply_split(behind[...], high[j], low[j])
        state = moved[:count] + source[i]
        forward[i] = state
        prefix[i] = moved[count:]
        ahead[:count] = state
        ahead[count:] = moved[count:]
        suffix[j] = back
        behind[...] = back
        return 0

    lax.fori_loop(0, rows, step, 0)
    operators[0] = ahead[count:]
    operators[1] = behind[...]
    ahead[...] = jnp.zeros_like(ahead)

    def back(i, _):
        j = rows - 1 - i
        entering = jnp.concatenate([forward[j], prefix[j]], axis=0) + ahead[...]
        state = apply_split(entering, high[j], low[j])
        ahead[...] = state
        solved[j] = state[:count]
        cross[j] = state[count:]
        return 0

    lax.fori_loop(0, rows, back, 0)
    operators[2] = ahead[count:]
    put_messages(ends, forward[rows - 1], ahead[:count], None)


def prepare(factors, source, copies):
    rows, width, _ = factors.shape
    count = source.shape[1]
    square = (rows, width, width)
    return call(
        prepare_body,
        [
            shape(*square, dtype=jnp.bfloat16),
            shape(*square, dtype=jnp.bfloat16),
            shape(*square),
            shape(*square),
            shape(*source.shape),
            shape(3, width, width),
            shape(copies, count + 8, width),
        ],
        [
            pltpu.VMEM(square, jnp.float32),
            pltpu.VMEM(source.shape, jnp.float32),
            pltpu.VMEM((count + width, width), jnp.float32),
            pltpu.VMEM((width, width), jnp.float32),
        ],
        rows * 6 * (2 * count + 3 * width) * width * width,
        factors,
        source,
    )


def ahead_body(high, low, cross, suffix, solved, rows_out, ends):
    rows, count, width = solved.shape
    ends[...] = jnp.zeros_like(ends)

    def step(i, _):
        source = jnp.concatenate([cross[i], suffix[i], solved[i]], axis=0)
        state = apply_split(ends[...], high[i], low[i]) + source
        ends[...] = state
        rows_out[i] = state
        return 0

    lax.fori_loop(0, rows, step, 0)


def behind_body(high, low, source, ends):
    rows = source.shape[0]
    ends[...] = jnp.zeros_like(ends)

    def step(i, _):
        j = rows - 1 - i
        ends[...] = apply_split(source[j] + ends[...], high[j], low[j])
        return 0

    lax.fori_loop(0, rows, step, 0)


def respond_ahead(high, low, cross, suffix, solved):
    rows, count, width = solved.shape
    length = 2 * width + count
    return call(
        ahead_body,
        [shape(rows, length, width), shape(length, width)],
        [],
        rows * 6 * length * width * width,
        high,
        low,
        cross,
        suffix,
        solved,
    )


def respond_behind(high, low, source, after):
    rows, length, width = source.shape
    return call(
        behind_body,
        [shape(length, width)],
        [],
        rows * 6 * length * width * width,
        high,
        low,
        source,
        after=after,
    )[0]


def identity(width):
    return (
        lax.broadcasted_iota(jnp.int32, (width, width), 0)
        == lax.broadcasted_iota(jnp.int32, (width, width), 1)
    ).astype(jnp.float32)


def row_span(spans, e, part):
    return spans[e, part]


def far_span(place, own, other, e, part):
    first = place[1] == 0
    return jnp.concatenate(
        [
            jnp.where(first, own[e, part], other[e, part]),
            jnp.where(first, other[e, part], own[e, part]),
        ],
        axis=0,
    )


def join_body(place, spans, own, half, reach, crossing):
    members, _, width, _ = spans.shape
    reach[0] = identity(width)
    reach[1] = identity(width)
    chip = place[0]
    kept = pl.ds(pl.multiple_of(place[1] * (width // 2), width // 2), width // 2)

    def outward(e, _):
        @pl.when(e // 2 == chip)
        def _():
            own[e % 2, 0] = reach[0]

        back = members - 1 - e

        @pl.when(back // 2 == chip)
        def _():
            own[back % 2, 1] = reach[1]

        ahead = reach[0]
        crossing[e] = apply_split(ahead, *split(spans[e, 2]))
        reach[1] = apply_split(reach[1], *split(spans[back, 1]))
        reach[0] = apply_split(ahead, *split(spans[e, 0]))
        return 0

    lax.fori_loop(0, members, outward, 0)
    half[0] = reach[0, kept]
    half[1] = reach[1, kept]
    reach[0] = jnp.zeros((width, width), jnp.float32)

    def inward(i, _):
        e = members - 1 - i

        @pl.when(e // 2 == chip)
        def _():
            own[e % 2, 2] = reach[0]

        reach[0] = apply_split(reach[0], *split(spans[e, 1])) + crossing[e]
        return 0

    lax.fori_loop(0, members, inward, 0)
    half[2] = reach[0, kept]


def join(place, spans, after):
    members, parts, width, _ = spans.shape
    return call(
        join_body,
        [shape(2, parts, width, width), shape(parts, width // 2, width)],
        [
            pltpu.VMEM((2, width, width), jnp.float32),
            pltpu.VMEM((members, width, width), jnp.float32),
        ],
        members * 6 * 4 * width**3,
        spans,
        after=after,
        position=place,
    )


def relay(span, ends, states):
    members, length, width = ends.shape
    count = (length - 8) // 2
    state = jnp.zeros((count, width), jnp.float32)
    entered = []
    for e in range(members):
        entered.append(state)
        states[0, e] = state
        end = ends[e, :count]
        state = end if e == 0 else apply_split(state, *split(span(e, 0))) + end
    ahead = state
    state = jnp.zeros((count, width), jnp.float32)
    for e in reversed(range(members)):
        states[1, e] = state
        end = ends[e, count : 2 * count]
        if e > 0:
            end = end + apply_split(entered[e], *split(span(e, 2)))
        state = end if e == members - 1 else apply_split(state, *split(span(e, 1))) + end
    return ahead, state


def total_of(ends):
    count = (ends.shape[1] - 8) // 2
    total = ends[0, 2 * count :]
    for e in range(1, ends.shape[0]):
        total = total + ends[e, 2 * count :]
    return total


def near_body(place, spans, ends, entered, messages, states):
    count = entered.shape[2]
    ahead, behind = relay(functools.partial(row_span, spans), ends, states)
    message = jnp.concatenate([ahead, behind, total_of(ends)], axis=0)
    for member in range(messages.shape[0]):
        messages[member] = message
    for core in range(2):
        for way in range(2):
            entered[core, way] = states[way, 2 * place[0] + core]


def near(place, spans, ends, copies):
    members, length, width = ends.shape
    count = (length - 8) // 2
    return call(
        near_body,
        [shape(2, 2, count, width), shape(copies, length, width)],
        [pltpu.VMEM((2, members, count, width), jnp.float32)],
        members * 6 * 3 * count * width * width,
        spans,
        ends,
        position=place,
    )


def far_body(place, spans, others, ends, own, inner, mine, theirs, squares, states, entering):
    relay(functools.partial(far_span, place, spans, others), ends, states)
    ahead, behind = states[0, place[0]], states[1, place[0]]
    for core in range(2):
        entering[core, 0] = apply_split(ahead, *split(own[core, 0])) + inner[core, 0]
        entering[core, 1] = (
            apply_split(behind, *split(own[core, 1]))
            + apply_split(ahead, *split(own[core, 2]))
            + inner[core, 1]
        )
    mine[...] = entering[place[1]]
    theirs[...] = entering[1 - place[1]]
    squares[...] = total_of(ends)


def far(place, spans, others, ends, own, inner):
    members, length, width = ends.shape
    count = (length - 8) // 2
    return call(
        far_body,
        [shape(2, count, width), shape(2, count, width), shape(8, width)],
        [
            pltpu.VMEM((2, members, count, width), jnp.float32),
            pltpu.VMEM((2, 2, count, width), jnp.float32),
        ],
        members * 6 * 3 * count * width * width,
        spans,
        others,
        ends,
        own,
        inner,
        position=place,
    )


def both_halves(place, mine, theirs, way):
    first = place[1] == 0
    return jnp.concatenate(
        [
            jnp.where(first, mine[way], theirs[way]),
            jnp.where(first, theirs[way], mine[way]),
        ],
        axis=0,
    )


def put_messages(messages, ahead, behind, sums):
    count = ahead.shape[0] // 2
    for member in range(messages.shape[0]):
        chosen = slice((member % 2) * count, (member % 2 + 1) * count)
        messages[member, :count] = ahead[chosen]
        messages[member, count : 2 * count] = behind[chosen]
        messages[member, 2 * count :] = jnp.zeros((8, messages.shape[2]), jnp.float32)
        if sums is not None:
            messages[member, 2 * count :, : 2 * count] = sums


def row_sums(total):
    ones = jnp.ones((8, total.shape[1]), jnp.float32)
    return lax.dot_general(
        ones,
        total,
        (((1,), (1,)), ((), ())),
        precision=lax.Precision.HIGHEST,
        preferred_element_type=jnp.float32,
    )


def first_body(place, high, low, source, mine, theirs, ahead_ends, behind_ends, solved, messages, forward):
    rows, count, width = source.shape
    entering = [both_halves(place, mine, theirs, way) for way in range(2)]

    def ahead(i, state):
        state = apply_split(state, high[i], low[i]) + source[i]
        forward[i] = state
        return state

    lax.fori_loop(0, rows, ahead, entering[0], unroll=2)

    def behind(i, carry):
        state, total = carry
        j = rows - 1 - i
        state = apply_split(forward[j] + state, high[j], low[j])
        solved[j] = state
        return state, total + state * state

    zero = jnp.zeros((count, width), jnp.float32)
    _, total = lax.fori_loop(0, rows, behind, (entering[1], zero), unroll=2)
    parts = [
        ends[2 * width :]
        + apply_split(entering[0], *split(ends[:width]))
        + apply_split(entering[1], *split(ends[width : 2 * width]))
        for ends in (ahead_ends, behind_ends)
    ]
    put_messages(messages, *parts, row_sums(total))


def first_rows(place, high, low, source, mine, theirs, ahead_ends, behind_ends, copies):
    rows, count, width = source.shape
    return call(
        first_body,
        [shape(*source.shape), shape(copies, count + 8, width)],
        [pltpu.VMEM(source.shape, jnp.float32)],
        2 * rows * 6 * count * width * width,
        high,
        low,
        source,
        mine,
        theirs,
        ahead_ends,
        behind_ends,
        position=place,
    )


def second_body(place, high, low, source, mine, theirs, scale, result, squares, forward):
    rows, count, width = source.shape
    inverse = 1.0 / scale[...]
    entering = [both_halves(place, mine, theirs, way) for way in range(2)]

    def ahead(i, state):
        state = apply_split(state, high[i], low[i]) + source[i]
        forward[i] = state
        return state

    lax.fori_loop(0, rows, ahead, entering[0], unroll=2)

    def behind(i, carry):
        state, total = carry
        j = rows - 1 - i
        state = apply_split(forward[j] + state, high[j], low[j])
        value = state * inverse
        result[j] = value
        return state, total + value * value

    zero = jnp.zeros((count, width), jnp.float32)
    _, total = lax.fori_loop(0, rows, behind, (entering[1], zero), unroll=2)
    squares[...] = jnp.zeros(squares.shape, jnp.float32)
    sums = row_sums(total)
    for member in range(squares.shape[0]):
        squares[member, :, :count] = sums


def second_rows(place, high, low, source, mine, theirs, scale, copies):
    rows, count, width = source.shape
    return call(
        second_body,
        [shape(*source.shape), shape(copies, 8, 128)],
        [pltpu.VMEM(source.shape, jnp.float32)],
        2 * rows * 6 * count * width * width,
        high,
        low,
        source,
        mine,
        theirs,
        scale,
        position=place,
    )


def scale_body(vectors, scale, result):
    result[...] = vectors[...] * (1.0 / scale[...])[None]


def rescale(vectors, scale):
    return call(scale_body, [shape(*vectors.shape)], [], vectors.size, vectors, scale)[0]


def swap(value, axis):
    return lax.all_to_all(value, axis, 0, 0, tiled=True)


def shards(start_vectors, factors):
    rows, count, width = start_vectors.shape
    cell_count = rows * lax.axis_size(CHAIN) * width
    members, groups = lax.axis_size(INNER), lax.axis_size("outer")
    core = lax.axis_index("core")
    near_place = jnp.stack([lax.axis_index("mid"), core]).astype(jnp.int32)
    far_place = jnp.stack([lax.axis_index("outer"), core]).astype(jnp.int32)
    cross_core = functools.partial(lax.ppermute, axis_name="core", perm=[(0, 1), (1, 0)])

    whole = lax.all_gather(factors, "cols", axis=1, tiled=True)
    high, low, suffix, cross, solved, operators, ends = prepare(whole, start_vectors, members)
    near_spans = lax.all_gather(operators, INNER)
    near_ends = swap(ends, INNER)
    ahead_rows, ahead_ends = respond_ahead(high, low, cross, suffix, solved)
    own, half = join(near_place, near_spans, (ahead_ends, near_ends))
    own_halves = lax.all_gather(half, "outer")
    behind_ends = respond_behind(high, low, ahead_rows, (own,))
    inner, message = near(near_place, near_spans, near_ends, groups)
    far_ends = swap(message, "outer")
    own_halves = gate(own_halves, (far_ends, behind_ends))
    far_spans = (own_halves, cross_core(own_halves))
    mine, theirs, _ = far(far_place, *far_spans, far_ends, own, inner)

    first_solve, message = first_rows(
        near_place,
        high,
        low,
        start_vectors,
        mine,
        cross_core(theirs),
        ahead_ends,
        behind_ends,
        members,
    )
    inner, message = near(near_place, near_spans, swap(message, INNER), groups)
    mine, theirs, squares = far(far_place, *far_spans, swap(message, "outer"), own, inner)
    scale_one = jnp.sqrt(squares[0, :count] / cell_count + eps_value)
    second, squares = second_rows(
        near_place, high, low, first_solve, mine, cross_core(theirs), scale_one[:, None], members
    )
    squares = jnp.sum(swap(squares, INNER), axis=0)
    squares = jnp.broadcast_to(squares[None], (groups, *squares.shape))
    squares = jnp.sum(swap(squares, "outer"), axis=0)
    scale_two = jnp.sqrt(squares[0, :count] / cell_count + eps_value)
    return rescale(second, scale_two[:, None]), jnp.log(scale_two)


def solution(mesh):
    size = mesh.shape["chain"]
    outer = 1 << ((size - 1).bit_length() // 2)
    devices = mesh.devices.reshape(outer, size // outer // 2, 2, mesh.shape["cols"])
    placed = P(CHAIN, "cols", None)
    return jax.shard_map(
        shards,
        mesh=Mesh(devices, (*CHAIN, "cols")),
        in_specs=(placed, placed),
        out_specs=(placed, P("cols")),
        check_vma=False,
    )
```

```python
import functools

import jax
import jax.numpy as jnp
from jax import lax
from jax.experimental import pallas as pl
from jax.experimental.pallas import tpu as pltpu
from jax.sharding import Mesh, PartitionSpec as P

eps_value = 1e-06
VMEM_BYTES = 56 * 1024 * 1024
INNER = ("mid", "core")
CHAIN = ("outer", *INNER)


def split(value):
    high = value.astype(jnp.bfloat16)
    low = (value - high.astype(jnp.float32)).astype(jnp.bfloat16)
    return high, low


def apply_split(state, high, low):
    rows = state.shape[0]
    state_high, state_low = split(state)
    both = jnp.dot(
        jnp.concatenate([state_high, state_low], axis=0),
        high,
        preferred_element_type=jnp.float32,
    )
    return (both[:rows] + both[rows:]) + jnp.dot(
        state_high, low, preferred_element_type=jnp.float32
    )


def call(body, out_shapes, scratch, flops, *operands, after=(), position=None):
    vmem = pl.BlockSpec(memory_space=pltpu.VMEM)
    touched = sum(x.size * x.dtype.itemsize for x in (*operands, *out_shapes))
    specs = [vmem] * len(operands)
    if position is not None:
        specs = [pl.BlockSpec(memory_space=pltpu.SMEM), *specs]
        operands = (position, *operands)
    kernel = body
    if after:
        specs = [pl.BlockSpec(memory_space=pl.ANY)] * len(after) + specs
        operands = (*after, *operands)

        def kernel(*refs):
            body(*refs[len(after) :])

    return pl.pallas_call(
        kernel,
        out_shape=tuple(out_shapes),
        in_specs=specs,
        out_specs=tuple([vmem] * len(out_shapes)),
        scratch_shapes=scratch,
        compiler_params=pltpu.CompilerParams(vmem_limit_bytes=VMEM_BYTES),
        cost_estimate=pl.CostEstimate(flops=flops, bytes_accessed=touched, transcendentals=0),
    )(*operands)


def shape(*dims, dtype=jnp.float32):
    return jax.ShapeDtypeStruct(dims, dtype)


def prepare_body(factors, source, high, low, suffix, cross, solved, operators, ends, prefix, forward, ahead, behind):
    rows, width, _ = factors.shape
    count = source.shape[1]

    def turn(i, _):
        high[i], low[i] = split(factors[i].T)
        return 0

    lax.fori_loop(0, rows, turn, 0)
    eye = identity(width)
    ahead[:count] = jnp.zeros((count, width), jnp.float32)
    ahead[count:] = eye
    behind[...] = eye

    def step(i, _):
        j = rows - 1 - i
        moved = apply_split(ahead[...], high[i], low[i])
        back = apply_split(behind[...], high[j], low[j])
        state = moved[:count] + source[i]
        forward[i] = state
        prefix[i] = moved[count:]
        ahead[:count] = state
        ahead[count:] = moved[count:]
        suffix[j] = back
        behind[...] = back
        return 0

    lax.fori_loop(0, rows, step, 0)
    operators[0] = ahead[count:]
    operators[1] = behind[...]
    ahead[...] = jnp.zeros_like(ahead)

    def back(i, _):
        j = rows - 1 - i
        entering = jnp.concatenate([forward[j], prefix[j]], axis=0) + ahead[...]
        state = apply_split(entering, high[j], low[j])
        ahead[...] = state
        solved[j] = state[:count]
        cross[j] = state[count:]
        return 0

    lax.fori_loop(0, rows, back, 0)
    operators[2] = ahead[count:]
    put_messages(ends, forward[rows - 1], ahead[:count], None)


def prepare(factors, source, copies):
    rows, width, _ = factors.shape
    count = source.shape[1]
    square = (rows, width, width)
    return call(
        prepare_body,
        [
            shape(*square, dtype=jnp.bfloat16),
            shape(*square, dtype=jnp.bfloat16),
            shape(*square),
            shape(*square),
            shape(*source.shape),
            shape(3, width, width),
            shape(copies, count + 8, width),
        ],
        [
            pltpu.VMEM(square, jnp.float32),
            pltpu.VMEM(source.shape, jnp.float32),
            pltpu.VMEM((count + width, width), jnp.float32),
            pltpu.VMEM((width, width), jnp.float32),
        ],
        rows * 6 * (2 * count + 3 * width) * width * width,
        factors,
        source,
    )


def ahead_body(high, low, cross, suffix, solved, rows_out, ends):
    rows, count, width = solved.shape
    ends[...] = jnp.zeros_like(ends)

    def step(i, _):
        source = jnp.concatenate([cross[i], suffix[i], solved[i]], axis=0)
        state = apply_split(ends[...], high[i], low[i]) + source
        ends[...] = state
        rows_out[i] = state
        return 0

    lax.fori_loop(0, rows, step, 0)


def behind_body(high, low, source, ends):
    rows = source.shape[0]
    ends[...] = jnp.zeros_like(ends)

    def step(i, _):
        j = rows - 1 - i
        ends[...] = apply_split(source[j] + ends[...], high[j], low[j])
        return 0

    lax.fori_loop(0, rows, step, 0)


def respond_ahead(high, low, cross, suffix, solved):
    rows, count, width = solved.shape
    length = 2 * width + count
    return call(
        ahead_body,
        [shape(rows, length, width), shape(length, width)],
        [],
        rows * 6 * length * width * width,
        high,
        low,
        cross,
        suffix,
        solved,
    )


def respond_behind(high, low, source, after):
    rows, length, width = source.shape
    return call(
        behind_body,
        [shape(length, width)],
        [],
        rows * 6 * length * width * width,
        high,
        low,
        source,
        after=after,
    )[0]


def identity(width):
    return (
        lax.broadcasted_iota(jnp.int32, (width, width), 0)
        == lax.broadcasted_iota(jnp.int32, (width, width), 1)
    ).astype(jnp.float32)


def row_span(spans, e, part):
    return spans[e, part]


def far_span(spans, e, part):
    return jnp.concatenate([spans[2 * e, part], spans[2 * e + 1, part]], axis=0)


def merge(before, behind):
    width = before[0].shape[0]
    ahead = apply_split(before[0], *split(behind[0]))
    turned = apply_split(before[0], *split(behind[2]))
    back = apply_split(jnp.concatenate([behind[1], turned], axis=0), *split(before[1]))
    return ahead, back[:width], before[2] + back[width:]


def compose_body(place, spans, half, whole):
    parts = spans.shape[1]
    width = spans.shape[2]
    level = [tuple(spans[e, part] for part in range(parts)) for e in range(spans.shape[0])]
    while len(level) > 1:
        level = [merge(*level[i : i + 2]) for i in range(0, len(level), 2)]
    kept = pl.ds(pl.multiple_of(place[1] * (width // 2), width // 2), width // 2)
    for part in range(parts):
        whole[...] = level[0][part]
        half[part] = whole[kept]


def compose(place, spans, after):
    members, parts, width, _ = spans.shape
    return call(
        compose_body,
        [shape(parts, width // 2, width)],
        [pltpu.VMEM((width, width), jnp.float32)],
        members * 6 * 4 * width**3,
        spans,
        after=after,
        position=place,
    )[0]


def reach_body(place, spans, own, reach, crossing):
    members, _, width, _ = spans.shape
    reach[0] = identity(width)
    reach[1] = identity(width)
    chip = place[0]

    def outward(e, _):
        @pl.when(e // 2 == chip)
        def _():
            own[e % 2, 0] = reach[0]

        back = members - 1 - e

        @pl.when(back // 2 == chip)
        def _():
            own[back % 2, 1] = reach[1]

        ahead = reach[0]
        crossing[e] = apply_split(ahead, *split(spans[e, 2]))
        reach[1] = apply_split(reach[1], *split(spans[back, 1]))
        reach[0] = apply_split(ahead, *split(spans[e, 0]))
        return 0

    lax.fori_loop(0, members, outward, 0)
    reach[0] = jnp.zeros((width, width), jnp.float32)

    def inward(i, _):
        e = members - 1 - i

        @pl.when(e // 2 == chip)
        def _():
            own[e % 2, 2] = reach[0]

        reach[0] = apply_split(reach[0], *split(spans[e, 1])) + crossing[e]
        return 0

    lax.fori_loop(0, members, inward, 0)


def reaching(place, spans, after):
    members, parts, width, _ = spans.shape
    return call(
        reach_body,
        [shape(2, parts, width, width)],
        [
            pltpu.VMEM((2, width, width), jnp.float32),
            pltpu.VMEM((members, width, width), jnp.float32),
        ],
        members * 6 * 4 * width**3,
        spans,
        after=after,
        position=place,
    )[0]


def relay(span, ends, states):
    members, length, width = ends.shape
    count = (length - 8) // 2
    state = jnp.zeros((count, width), jnp.float32)
    entered = []
    for e in range(members):
        entered.append(state)
        states[0, e] = state
        end = ends[e, :count]
        state = end if e == 0 else apply_split(state, *split(span(e, 0))) + end
    ahead = state
    state = jnp.zeros((count, width), jnp.float32)
    for e in reversed(range(members)):
        states[1, e] = state
        end = ends[e, count : 2 * count]
        if e > 0:
            end = end + apply_split(entered[e], *split(span(e, 2)))
        state = end if e == members - 1 else apply_split(state, *split(span(e, 1))) + end
    return ahead, state


def total_of(ends):
    count = (ends.shape[1] - 8) // 2
    total = ends[0, 2 * count :]
    for e in range(1, ends.shape[0]):
        total = total + ends[e, 2 * count :]
    return total


def near_body(place, spans, ends, entered, messages, states):
    count = entered.shape[2]
    ahead, behind = relay(functools.partial(row_span, spans), ends, states)
    message = jnp.concatenate([ahead, behind, total_of(ends)], axis=0)
    for member in range(messages.shape[0]):
        messages[member] = message
    for core in range(2):
        for way in range(2):
            entered[core, way] = states[way, 2 * place[0] + core]


def near(place, spans, ends, copies):
    members, length, width = ends.shape
    count = (length - 8) // 2
    return call(
        near_body,
        [shape(2, 2, count, width), shape(copies, length, width)],
        [pltpu.VMEM((2, members, count, width), jnp.float32)],
        members * 6 * 3 * count * width * width,
        spans,
        ends,
        position=place,
    )


def far_body(place, spans, ends, own, inner, mine, theirs, squares, states, entering):
    relay(functools.partial(far_span, spans), ends, states)
    ahead, behind = states[0, place[0]], states[1, place[0]]
    for core in range(2):
        entering[core, 0] = apply_split(ahead, *split(own[core, 0])) + inner[core, 0]
        entering[core, 1] = (
            apply_split(behind, *split(own[core, 1]))
            + apply_split(ahead, *split(own[core, 2]))
            + inner[core, 1]
        )
    mine[...] = entering[place[1]]
    theirs[...] = entering[1 - place[1]]
    squares[...] = total_of(ends)


def far(place, spans, ends, own, inner, after=()):
    members, length, width = ends.shape
    count = (length - 8) // 2
    return call(
        far_body,
        [shape(2, count, width), shape(2, count, width), shape(8, width)],
        [
            pltpu.VMEM((2, members, count, width), jnp.float32),
            pltpu.VMEM((2, 2, count, width), jnp.float32),
        ],
        members * 6 * 3 * count * width * width,
        spans,
        ends,
        own,
        inner,
        after=after,
        position=place,
    )


def both_halves(place, mine, theirs, way):
    first = place[1] == 0
    return jnp.concatenate(
        [
            jnp.where(first, mine[way], theirs[way]),
            jnp.where(first, theirs[way], mine[way]),
        ],
        axis=0,
    )


def put_messages(messages, ahead, behind, sums):
    count = ahead.shape[0] // 2
    for member in range(messages.shape[0]):
        chosen = slice((member % 2) * count, (member % 2 + 1) * count)
        messages[member, :count] = ahead[chosen]
        messages[member, count : 2 * count] = behind[chosen]
        messages[member, 2 * count :] = jnp.zeros((8, messages.shape[2]), jnp.float32)
        if sums is not None:
            messages[member, 2 * count :, : 2 * count] = sums


def row_sums(total):
    ones = jnp.ones((8, total.shape[1]), jnp.float32)
    return lax.dot_general(
        ones,
        total,
        (((1,), (1,)), ((), ())),
        precision=lax.Precision.HIGHEST,
        preferred_element_type=jnp.float32,
    )


def first_body(place, high, low, source, mine, theirs, ahead_ends, behind_ends, solved, messages, forward):
    rows, count, width = source.shape
    entering = [both_halves(place, mine, theirs, way) for way in range(2)]

    def ahead(i, state):
        state = apply_split(state, high[i], low[i]) + source[i]
        forward[i] = state
        return state

    lax.fori_loop(0, rows, ahead, entering[0], unroll=2)

    def behind(i, carry):
        state, total = carry
        j = rows - 1 - i
        state = apply_split(forward[j] + state, high[j], low[j])
        solved[j] = state
        return state, total + state * state

    zero = jnp.zeros((count, width), jnp.float32)
    _, total = lax.fori_loop(0, rows, behind, (entering[1], zero), unroll=2)
    parts = [
        ends[2 * width :]
        + apply_split(entering[0], *split(ends[:width]))
        + apply_split(entering[1], *split(ends[width : 2 * width]))
        for ends in (ahead_ends, behind_ends)
    ]
    put_messages(messages, *parts, row_sums(total))


def first_rows(place, high, low, source, mine, theirs, ahead_ends, behind_ends, copies):
    rows, count, width = source.shape
    return call(
        first_body,
        [shape(*source.shape), shape(copies, count + 8, width)],
        [pltpu.VMEM(source.shape, jnp.float32)],
        2 * rows * 6 * count * width * width,
        high,
        low,
        source,
        mine,
        theirs,
        ahead_ends,
        behind_ends,
        position=place,
    )


def second_body(place, high, low, source, mine, theirs, scale, result, squares, forward):
    rows, count, width = source.shape
    inverse = 1.0 / scale[...]
    entering = [both_halves(place, mine, theirs, way) for way in range(2)]

    def ahead(i, state):
        state = apply_split(state, high[i], low[i]) + source[i]
        forward[i] = state
        return state

    lax.fori_loop(0, rows, ahead, entering[0], unroll=2)

    def behind(i, carry):
        state, total = carry
        j = rows - 1 - i
        state = apply_split(forward[j] + state, high[j], low[j])
        value = state * inverse
        result[j] = value
        return state, total + value * value

    zero = jnp.zeros((count, width), jnp.float32)
    _, total = lax.fori_loop(0, rows, behind, (entering[1], zero), unroll=2)
    squares[...] = jnp.zeros(squares.shape, jnp.float32)
    sums = row_sums(total)
    for member in range(squares.shape[0]):
        squares[member, :, :count] = sums


def second_rows(place, high, low, source, mine, theirs, scale, copies):
    rows, count, width = source.shape
    return call(
        second_body,
        [shape(*source.shape), shape(copies, 8, 128)],
        [pltpu.VMEM(source.shape, jnp.float32)],
        2 * rows * 6 * count * width * width,
        high,
        low,
        source,
        mine,
        theirs,
        scale,
        position=place,
    )


def scale_body(vectors, scale, result):
    result[...] = vectors[...] * (1.0 / scale[...])[None]


def rescale(vectors, scale):
    return call(scale_body, [shape(*vectors.shape)], [], vectors.size, vectors, scale)[0]


def swap(value, axis):
    return lax.all_to_all(value, axis, 0, 0, tiled=True)


def shards(start_vectors, factors):
    rows, count, width = start_vectors.shape
    cell_count = rows * lax.axis_size(CHAIN) * width
    members, groups = lax.axis_size(INNER), lax.axis_size("outer")
    core = lax.axis_index("core")
    near_place = jnp.stack([lax.axis_index("mid"), core]).astype(jnp.int32)
    far_place = jnp.stack([lax.axis_index("outer"), core]).astype(jnp.int32)
    cross_core = functools.partial(lax.ppermute, axis_name="core", perm=[(0, 1), (1, 0)])

    whole = lax.all_gather(factors, "cols", axis=1, tiled=True)
    high, low, suffix, cross, solved, operators, ends = prepare(whole, start_vectors, members)
    near_spans = lax.all_gather(operators, INNER)
    near_ends = swap(ends, INNER)
    ahead_rows, ahead_ends = respond_ahead(high, low, cross, suffix, solved)
    half = compose(near_place, near_spans, (ahead_ends, near_ends))
    far_spans = lax.all_gather(half, ("outer", "core"))
    inner, message = near(near_place, near_spans, near_ends, groups)
    far_ends = swap(message, "outer")
    behind_ends = respond_behind(high, low, ahead_rows, (half,))
    own = reaching(near_place, near_spans, (half,))
    mine, theirs, _ = far(far_place, far_spans, far_ends, own, inner, (behind_ends,))

    first_solve, message = first_rows(
        near_place,
        high,
        low,
        start_vectors,
        mine,
        cross_core(theirs),
        ahead_ends,
        behind_ends,
        members,
    )
    inner, message = near(near_place, near_spans, swap(message, INNER), groups)
    mine, theirs, squares = far(far_place, far_spans, swap(message, "outer"), own, inner)
    scale_one = jnp.sqrt(squares[0, :count] / cell_count + eps_value)
    second, squares = second_rows(
        near_place, high, low, first_solve, mine, cross_core(theirs), scale_one[:, None], members
    )
    squares = jnp.sum(swap(squares, INNER), axis=0)
    squares = jnp.broadcast_to(squares[None], (groups, *squares.shape))
    squares = jnp.sum(swap(squares, "outer"), axis=0)
    scale_two = jnp.sqrt(squares[0, :count] / cell_count + eps_value)
    return rescale(second, scale_two[:, None]), jnp.log(scale_two)


def solution(mesh):
    size = mesh.shape["chain"]
    outer = 1 << ((size - 1).bit_length() // 2)
    devices = mesh.devices.reshape(outer, size // outer // 2, 2, mesh.shape["cols"])
    placed = P(CHAIN, "cols", None)
    return jax.shard_map(
        shards,
        mesh=Mesh(devices, (*CHAIN, "cols")),
        in_specs=(placed, placed),
        out_specs=(placed, P("cols")),
        check_vma=False,
    )
```

```python
import functools

import jax
import jax.numpy as jnp
from jax import lax
from jax.experimental import pallas as pl
from jax.experimental.pallas import tpu as pltpu
from jax.sharding import Mesh, PartitionSpec as P

eps_value = 1e-06
VMEM_BYTES = 56 * 1024 * 1024
INNER = ("mid", "core")
CHAIN = ("outer", *INNER)


def split(value):
    high = value.astype(jnp.bfloat16)
    low = (value - high.astype(jnp.float32)).astype(jnp.bfloat16)
    return high, low


def apply_split(state, high, low):
    rows = state.shape[0]
    state_high, state_low = split(state)
    both = jnp.dot(
        jnp.concatenate([state_high, state_low], axis=0),
        high,
        preferred_element_type=jnp.float32,
    )
    return (both[:rows] + both[rows:]) + jnp.dot(
        state_high, low, preferred_element_type=jnp.float32
    )


class Streamed:
    def __init__(self, source, buffer, done):
        self.source, self.buffer, self.done = source, buffer, done
        self.shape = buffer.shape

    def copy(self, block):
        return pltpu.make_async_copy(
            self.source.at[block], self.buffer.at[block], self.done.at[block]
        )

    def wait(self, block):
        self.copy(block).wait()

    def __getitem__(self, index):
        return self.buffer[index]


def call(body, out_shapes, scratch, flops, *operands, after=(), position=None, streamed=()):
    vmem = pl.BlockSpec(memory_space=pltpu.VMEM)
    anywhere = pl.BlockSpec(memory_space=pl.ANY)
    touched = sum(x.size * x.dtype.itemsize for x in (*operands, *out_shapes))
    specs = [anywhere if i in streamed else vmem for i in range(len(operands))]
    buffers = [pltpu.VMEM(operands[i].shape, operands[i].dtype) for i in streamed]
    done = [pltpu.SemaphoreType.DMA((operands[i].shape[0],)) for i in streamed]
    first = 0
    if position is not None:
        specs = [pl.BlockSpec(memory_space=pltpu.SMEM), *specs]
        operands = (position, *operands)
        first = 1
    specs = [anywhere] * len(after) + specs

    def kernel(*refs):
        refs = list(refs[len(after) :])
        ends = len(refs) - 2 * len(streamed)
        extra = refs[ends:]
        refs = refs[:ends]
        arriving = []
        for k, i in enumerate(streamed):
            refs[first + i] = Streamed(refs[first + i], extra[k], extra[len(streamed) + k])
            arriving.append(refs[first + i])
        if arriving:
            for block in range(arriving[0].shape[0]):
                for operand in arriving:
                    operand.copy(block).start()
        body(*refs)

    return pl.pallas_call(
        kernel,
        out_shape=tuple(out_shapes),
        in_specs=specs,
        out_specs=tuple([vmem] * len(out_shapes)),
        scratch_shapes=[*scratch, *buffers, *done],
        compiler_params=pltpu.CompilerParams(vmem_limit_bytes=VMEM_BYTES),
        cost_estimate=pl.CostEstimate(flops=flops, bytes_accessed=touched, transcendentals=0),
    )(*after, *operands)


def shape(*dims, dtype=jnp.float32):
    return jax.ShapeDtypeStruct(dims, dtype)


def prepare_body(factors, source, high, low, suffix, cross, solved, operators, ends, prefix, forward, ahead, behind):
    rows, width, _ = factors.shape
    count = source.shape[1]

    def turn(i, _):
        factors.wait(i)
        high[i], low[i] = split(factors[i].T)
        return 0

    lax.fori_loop(0, rows, turn, 0)
    eye = identity(width)
    ahead[:count] = jnp.zeros((count, width), jnp.float32)
    ahead[count:] = eye
    behind[...] = eye

    def step(i, _):
        j = rows - 1 - i
        moved = apply_split(ahead[...], high[i], low[i])
        back = apply_split(behind[...], high[j], low[j])
        state = moved[:count] + source[i]
        forward[i] = state
        prefix[i] = moved[count:]
        ahead[:count] = state
        ahead[count:] = moved[count:]
        suffix[j] = back
        behind[...] = back
        return 0

    lax.fori_loop(0, rows, step, 0)
    operators[0] = ahead[count:]
    operators[1] = behind[...]
    ahead[...] = jnp.zeros_like(ahead)

    def back(i, _):
        j = rows - 1 - i
        entering = jnp.concatenate([forward[j], prefix[j]], axis=0) + ahead[...]
        state = apply_split(entering, high[j], low[j])
        ahead[...] = state
        solved[j] = state[:count]
        cross[j] = state[count:]
        return 0

    lax.fori_loop(0, rows, back, 0)
    operators[2] = ahead[count:]
    put_messages(ends, forward[rows - 1], ahead[:count], None)


def prepare(factors, source, copies):
    rows, width, _ = factors.shape
    count = source.shape[1]
    square = (rows, width, width)
    return call(
        prepare_body,
        [
            shape(*square, dtype=jnp.bfloat16),
            shape(*square, dtype=jnp.bfloat16),
            shape(*square),
            shape(*square),
            shape(*source.shape),
            shape(3, width, width),
            shape(copies, count + 8, width),
        ],
        [
            pltpu.VMEM(square, jnp.float32),
            pltpu.VMEM(source.shape, jnp.float32),
            pltpu.VMEM((count + width, width), jnp.float32),
            pltpu.VMEM((width, width), jnp.float32),
        ],
        rows * 6 * (2 * count + 3 * width) * width * width,
        factors,
        source,
        streamed=(0,),
    )


def ahead_body(high, low, cross, suffix, solved, rows_out, ends):
    rows, count, width = solved.shape
    ends[...] = jnp.zeros_like(ends)

    def step(i, _):
        source = jnp.concatenate([cross[i], suffix[i], solved[i]], axis=0)
        state = apply_split(ends[...], high[i], low[i]) + source
        ends[...] = state
        rows_out[i] = state
        return 0

    lax.fori_loop(0, rows, step, 0)


def behind_body(high, low, source, ends):
    rows = source.shape[0]
    ends[...] = jnp.zeros_like(ends)

    def step(i, _):
        j = rows - 1 - i
        ends[...] = apply_split(source[j] + ends[...], high[j], low[j])
        return 0

    lax.fori_loop(0, rows, step, 0)


def respond_ahead(high, low, cross, suffix, solved):
    rows, count, width = solved.shape
    length = 2 * width + count
    return call(
        ahead_body,
        [shape(rows, length, width), shape(length, width)],
        [],
        rows * 6 * length * width * width,
        high,
        low,
        cross,
        suffix,
        solved,
    )


def respond_behind(high, low, source, after):
    rows, length, width = source.shape
    return call(
        behind_body,
        [shape(length, width)],
        [],
        rows * 6 * length * width * width,
        high,
        low,
        source,
        after=after,
    )[0]


def identity(width):
    return (
        lax.broadcasted_iota(jnp.int32, (width, width), 0)
        == lax.broadcasted_iota(jnp.int32, (width, width), 1)
    ).astype(jnp.float32)


def row_span(spans, e, part):
    return spans[e, part]


def far_span(spans, e, part):
    return jnp.concatenate([spans[2 * e, part], spans[2 * e + 1, part]], axis=0)


def merge(before, behind):
    width = before[0].shape[0]
    ahead = apply_split(before[0], *split(behind[0]))
    turned = apply_split(before[0], *split(behind[2]))
    back = apply_split(jnp.concatenate([behind[1], turned], axis=0), *split(before[1]))
    return ahead, back[:width], before[2] + back[width:]


def compose_body(place, spans, half, whole):
    parts = spans.shape[1]
    width = spans.shape[2]

    def span(e):
        spans.wait(e)
        return tuple(spans[e, part] for part in range(parts))

    level = [merge(span(e), span(e + 1)) for e in range(0, spans.shape[0], 2)]
    while len(level) > 1:
        level = [merge(*level[i : i + 2]) for i in range(0, len(level), 2)]
    kept = pl.ds(pl.multiple_of(place[1] * (width // 2), width // 2), width // 2)
    for part in range(parts):
        whole[...] = level[0][part]
        half[part] = whole[kept]


def compose(place, spans, after):
    members, parts, width, _ = spans.shape
    return call(
        compose_body,
        [shape(parts, width // 2, width)],
        [pltpu.VMEM((width, width), jnp.float32)],
        members * 6 * 4 * width**3,
        spans,
        after=after,
        position=place,
        streamed=(0,),
    )[0]


def reach_body(place, spans, own, reach, crossing):
    members, _, width, _ = spans.shape
    reach[0] = identity(width)
    reach[1] = identity(width)
    chip = place[0]

    def outward(e, _):
        @pl.when(e // 2 == chip)
        def _():
            own[e % 2, 0] = reach[0]

        back = members - 1 - e

        @pl.when(back // 2 == chip)
        def _():
            own[back % 2, 1] = reach[1]

        ahead = reach[0]
        crossing[e] = apply_split(ahead, *split(spans[e, 2]))
        reach[1] = apply_split(reach[1], *split(spans[back, 1]))
        reach[0] = apply_split(ahead, *split(spans[e, 0]))
        return 0

    lax.fori_loop(0, members, outward, 0)
    reach[0] = jnp.zeros((width, width), jnp.float32)

    def inward(i, _):
        e = members - 1 - i

        @pl.when(e // 2 == chip)
        def _():
            own[e % 2, 2] = reach[0]

        reach[0] = apply_split(reach[0], *split(spans[e, 1])) + crossing[e]
        return 0

    lax.fori_loop(0, members, inward, 0)


def reaching(place, spans, after):
    members, parts, width, _ = spans.shape
    return call(
        reach_body,
        [shape(2, parts, width, width)],
        [
            pltpu.VMEM((2, width, width), jnp.float32),
            pltpu.VMEM((members, width, width), jnp.float32),
        ],
        members * 6 * 4 * width**3,
        spans,
        after=after,
        position=place,
    )[0]


def relay(span, arrive, ends, states):
    members, length, width = ends.shape
    count = (length - 8) // 2
    state = jnp.zeros((count, width), jnp.float32)
    entered = []
    for e in range(members):
        arrive(e)
        entered.append(state)
        states[0, e] = state
        end = ends[e, :count]
        state = end if e == 0 else apply_split(state, *split(span(e, 0))) + end
    ahead = state
    state = jnp.zeros((count, width), jnp.float32)
    for e in reversed(range(members)):
        states[1, e] = state
        end = ends[e, count : 2 * count]
        if e > 0:
            end = end + apply_split(entered[e], *split(span(e, 2)))
        state = end if e == members - 1 else apply_split(state, *split(span(e, 1))) + end
    return ahead, state


def total_of(ends):
    count = (ends.shape[1] - 8) // 2
    total = ends[0, 2 * count :]
    for e in range(1, ends.shape[0]):
        total = total + ends[e, 2 * count :]
    return total


def near_body(place, spans, ends, entered, messages, states):
    count = entered.shape[2]
    ahead, behind = relay(functools.partial(row_span, spans), spans.wait, ends, states)
    message = jnp.concatenate([ahead, behind, total_of(ends)], axis=0)
    for member in range(messages.shape[0]):
        messages[member] = message
    for core in range(2):
        for way in range(2):
            entered[core, way] = states[way, 2 * place[0] + core]


def near(place, spans, ends, copies):
    members, length, width = ends.shape
    count = (length - 8) // 2
    return call(
        near_body,
        [shape(2, 2, count, width), shape(copies, length, width)],
        [pltpu.VMEM((2, members, count, width), jnp.float32)],
        members * 6 * 3 * count * width * width,
        spans,
        ends,
        position=place,
        streamed=(0,),
    )


def far_body(place, spans, ends, own, inner, mine, theirs, squares, states, entering):

    def arrive(e):
        spans.wait(2 * e)
        spans.wait(2 * e + 1)

    relay(functools.partial(far_span, spans), arrive, ends, states)
    ahead, behind = states[0, place[0]], states[1, place[0]]
    for core in range(2):
        entering[core, 0] = apply_split(ahead, *split(own[core, 0])) + inner[core, 0]
        entering[core, 1] = (
            apply_split(behind, *split(own[core, 1]))
            + apply_split(ahead, *split(own[core, 2]))
            + inner[core, 1]
        )
    mine[...] = entering[place[1]]
    theirs[...] = entering[1 - place[1]]
    squares[...] = total_of(ends)


def far(place, spans, ends, own, inner, after=()):
    members, length, width = ends.shape
    count = (length - 8) // 2
    return call(
        far_body,
        [shape(2, count, width), shape(2, count, width), shape(8, width)],
        [
            pltpu.VMEM((2, members, count, width), jnp.float32),
            pltpu.VMEM((2, 2, count, width), jnp.float32),
        ],
        members * 6 * 3 * count * width * width,
        spans,
        ends,
        own,
        inner,
        after=after,
        position=place,
        streamed=(0,),
    )


def both_halves(place, mine, theirs, way):
    first = place[1] == 0
    return jnp.concatenate(
        [
            jnp.where(first, mine[way], theirs[way]),
            jnp.where(first, theirs[way], mine[way]),
        ],
        axis=0,
    )


def put_messages(messages, ahead, behind, sums):
    count = ahead.shape[0] // 2
    for member in range(messages.shape[0]):
        chosen = slice((member % 2) * count, (member % 2 + 1) * count)
        messages[member, :count] = ahead[chosen]
        messages[member, count : 2 * count] = behind[chosen]
        messages[member, 2 * count :] = jnp.zeros((8, messages.shape[2]), jnp.float32)
        if sums is not None:
            messages[member, 2 * count :, : 2 * count] = sums


def row_sums(total):
    ones = jnp.ones((8, total.shape[1]), jnp.float32)
    return lax.dot_general(
        ones,
        total,
        (((1,), (1,)), ((), ())),
        precision=lax.Precision.HIGHEST,
        preferred_element_type=jnp.float32,
    )


def first_body(place, high, low, source, mine, theirs, ahead_ends, behind_ends, solved, messages, forward):
    rows, count, width = source.shape
    entering = [both_halves(place, mine, theirs, way) for way in range(2)]

    def ahead(i, state):
        high.wait(i)
        low.wait(i)
        state = apply_split(state, high[i], low[i]) + source[i]
        forward[i] = state
        return state

    lax.fori_loop(0, rows, ahead, entering[0], unroll=2)

    def behind(i, carry):
        state, total = carry
        j = rows - 1 - i
        state = apply_split(forward[j] + state, high[j], low[j])
        solved[j] = state
        return state, total + state * state

    zero = jnp.zeros((count, width), jnp.float32)
    _, total = lax.fori_loop(0, rows, behind, (entering[1], zero), unroll=2)
    parts = [
        ends[2 * width :]
        + apply_split(entering[0], *split(ends[:width]))
        + apply_split(entering[1], *split(ends[width : 2 * width]))
        for ends in (ahead_ends, behind_ends)
    ]
    put_messages(messages, *parts, row_sums(total))


def first_rows(place, high, low, source, mine, theirs, ahead_ends, behind_ends, copies):
    rows, count, width = source.shape
    return call(
        first_body,
        [shape(*source.shape), shape(copies, count + 8, width)],
        [pltpu.VMEM(source.shape, jnp.float32)],
        2 * rows * 6 * count * width * width,
        high,
        low,
        source,
        mine,
        theirs,
        ahead_ends,
        behind_ends,
        position=place,
        streamed=(0, 1),
    )


def second_body(place, high, low, source, mine, theirs, scale, result, squares, forward):
    rows, count, width = source.shape
    inverse = 1.0 / scale[...]
    entering = [both_halves(place, mine, theirs, way) for way in range(2)]

    def ahead(i, state):
        high.wait(i)
        low.wait(i)
        state = apply_split(state, high[i], low[i]) + source[i]
        forward[i] = state
        return state

    lax.fori_loop(0, rows, ahead, entering[0], unroll=2)

    def behind(i, carry):
        state, total = carry
        j = rows - 1 - i
        state = apply_split(forward[j] + state, high[j], low[j])
        value = state * inverse
        result[j] = value
        return state, total + value * value

    zero = jnp.zeros((count, width), jnp.float32)
    _, total = lax.fori_loop(0, rows, behind, (entering[1], zero), unroll=2)
    squares[...] = jnp.zeros(squares.shape, jnp.float32)
    sums = row_sums(total)
    for member in range(squares.shape[0]):
        squares[member, :, :count] = sums


def second_rows(place, high, low, source, mine, theirs, scale, copies):
    rows, count, width = source.shape
    return call(
        second_body,
        [shape(*source.shape), shape(copies, 8, 128)],
        [pltpu.VMEM(source.shape, jnp.float32)],
        2 * rows * 6 * count * width * width,
        high,
        low,
        source,
        mine,
        theirs,
        scale,
        position=place,
        streamed=(0, 1),
    )


def scale_body(vectors, scale, result):
    result[...] = vectors[...] * (1.0 / scale[...])[None]


def rescale(vectors, scale):
    return call(scale_body, [shape(*vectors.shape)], [], vectors.size, vectors, scale)[0]


def swap(value, axis):
    return lax.all_to_all(value, axis, 0, 0, tiled=True)


def shards(start_vectors, factors):
    rows, count, width = start_vectors.shape
    cell_count = rows * lax.axis_size(CHAIN) * width
    members, groups = lax.axis_size(INNER), lax.axis_size("outer")
    core = lax.axis_index("core")
    near_place = jnp.stack([lax.axis_index("mid"), core]).astype(jnp.int32)
    far_place = jnp.stack([lax.axis_index("outer"), core]).astype(jnp.int32)
    cross_core = functools.partial(lax.ppermute, axis_name="core", perm=[(0, 1), (1, 0)])

    whole = lax.all_gather(factors, "cols", axis=1, tiled=True)
    high, low, suffix, cross, solved, operators, ends = prepare(whole, start_vectors, members)
    near_spans = lax.all_gather(operators, INNER)
    near_ends = swap(ends, INNER)
    ahead_rows, ahead_ends = respond_ahead(high, low, cross, suffix, solved)
    half = compose(near_place, near_spans, (ahead_ends, near_ends))
    far_spans = lax.all_gather(half, ("outer", "core"))
    inner, message = near(near_place, near_spans, near_ends, groups)
    far_ends = swap(message, "outer")
    behind_ends = respond_behind(high, low, ahead_rows, (half,))
    own = reaching(near_place, near_spans, (half,))
    mine, theirs, _ = far(far_place, far_spans, far_ends, own, inner, (behind_ends,))

    first_solve, message = first_rows(
        near_place,
        high,
        low,
        start_vectors,
        mine,
        cross_core(theirs),
        ahead_ends,
        behind_ends,
        members,
    )
    inner, message = near(near_place, near_spans, swap(message, INNER), groups)
    mine, theirs, squares = far(far_place, far_spans, swap(message, "outer"), own, inner)
    scale_one = jnp.sqrt(squares[0, :count] / cell_count + eps_value)
    second, squares = second_rows(
        near_place, high, low, first_solve, mine, cross_core(theirs), scale_one[:, None], members
    )
    squares = jnp.sum(swap(squares, INNER), axis=0)
    squares = jnp.broadcast_to(squares[None], (groups, *squares.shape))
    squares = jnp.sum(swap(squares, "outer"), axis=0)
    scale_two = jnp.sqrt(squares[0, :count] / cell_count + eps_value)
    return rescale(second, scale_two[:, None]), jnp.log(scale_two)


def solution(mesh):
    size = mesh.shape["chain"]
    outer = 1 << ((size - 1).bit_length() // 2)
    devices = mesh.devices.reshape(outer, size // outer // 2, 2, mesh.shape["cols"])
    placed = P(CHAIN, "cols", None)
    return jax.shard_map(
        shards,
        mesh=Mesh(devices, (*CHAIN, "cols")),
        in_specs=(placed, placed),
        out_specs=(placed, P("cols")),
        check_vma=False,
    )
```

```python
import functools

import jax
import jax.numpy as jnp
from jax import lax
from jax.experimental import pallas as pl
from jax.experimental.pallas import tpu as pltpu
from jax.sharding import Mesh, PartitionSpec as P

eps_value = 1e-06
VMEM_BYTES = 56 * 1024 * 1024
INNER = ("mid", "core")
CHAIN = ("outer", *INNER)


def split(value):
    high = value.astype(jnp.bfloat16)
    low = (value - high.astype(jnp.float32)).astype(jnp.bfloat16)
    return high, low


def apply_split(state, high, low):
    rows = state.shape[0]
    state_high, state_low = split(state)
    both = jnp.dot(
        jnp.concatenate([state_high, state_low], axis=0),
        high,
        preferred_element_type=jnp.float32,
    )
    return (both[:rows] + both[rows:]) + jnp.dot(
        state_high, low, preferred_element_type=jnp.float32
    )


def call(body, out_shapes, scratch, flops, *operands, after=(), position=None):
    vmem = pl.BlockSpec(memory_space=pltpu.VMEM)
    touched = sum(x.size * x.dtype.itemsize for x in (*operands, *out_shapes))
    specs = [vmem] * len(operands)
    if position is not None:
        specs = [pl.BlockSpec(memory_space=pltpu.SMEM), *specs]
        operands = (position, *operands)
    kernel = body
    if after:
        specs = [pl.BlockSpec(memory_space=pl.ANY)] * len(after) + specs
        operands = (*after, *operands)

        def kernel(*refs):
            body(*refs[len(after) :])

    return pl.pallas_call(
        kernel,
        out_shape=tuple(out_shapes),
        in_specs=specs,
        out_specs=tuple([vmem] * len(out_shapes)),
        scratch_shapes=scratch,
        compiler_params=pltpu.CompilerParams(vmem_limit_bytes=VMEM_BYTES),
        cost_estimate=pl.CostEstimate(flops=flops, bytes_accessed=touched, transcendentals=0),
    )(*operands)


def shape(*dims, dtype=jnp.float32):
    return jax.ShapeDtypeStruct(dims, dtype)


def prepare_body(factors, source, high, low, prefix, forward, operators, ends, ahead, back, behind):
    rows, width, _ = factors.shape
    count = source.shape[1]
    ahead[:count] = jnp.zeros((count, width), jnp.float32)
    ahead[count:] = identity(width)
    behind[...] = jnp.zeros_like(behind)
    back[0], back[1] = split(identity(width))

    def step(i, _):
        turned = split(factors[i].T)
        high[i], low[i] = turned
        both = jnp.dot(
            jnp.concatenate(turned, axis=0), back[0], preferred_element_type=jnp.float32
        )
        through = (both[:width] + both[width:]) + jnp.dot(
            turned[0], back[1], preferred_element_type=jnp.float32
        )
        moved = apply_split(ahead[...], *turned)
        state = moved[:count] + source[i]
        forward[i] = state
        prefix[i] = moved[count:]
        ahead[:count] = state
        ahead[count:] = moved[count:]
        back[0], back[1] = split(through)
        operators[1] = through
        behind[...] += apply_split(ahead[...], back[0], back[1])
        return 0

    lax.fori_loop(0, rows, step, 0, unroll=8)
    operators[0] = ahead[count:]
    operators[2] = behind[count:]
    put_messages(ends, ahead[:count], behind[:count], None)


def prepare(factors, source, copies):
    rows, width, _ = factors.shape
    count = source.shape[1]
    square = (rows, width, width)
    return call(
        prepare_body,
        [
            shape(*square, dtype=jnp.bfloat16),
            shape(*square, dtype=jnp.bfloat16),
            shape(*square),
            shape(*source.shape),
            shape(3, width, width),
            shape(copies, count + 8, width),
        ],
        [
            pltpu.VMEM((count + width, width), jnp.float32),
            pltpu.VMEM((2, width, width), jnp.bfloat16),
            pltpu.VMEM((count + width, width), jnp.float32),
        ],
        rows * 6 * (2 * count + 3 * width) * width * width,
        factors,
        source,
    )


def ahead_body(high, low, prefix, forward, rows_out, ends):
    rows, count, width = forward.shape
    zero = jnp.zeros((width, width), jnp.float32)
    ends[:width] = zero
    ends[width : 2 * width] = identity(width)
    ends[2 * width :] = jnp.zeros((count, width), jnp.float32)

    def back(i, _):
        j = rows - 1 - i
        source = jnp.concatenate([prefix[j], zero, forward[j]], axis=0)
        state = apply_split(source + ends[...], high[j], low[j])
        ends[...] = state
        rows_out[j] = state
        return 0

    lax.fori_loop(0, rows, back, 0)
    ends[...] = jnp.zeros_like(ends)

    def step(i, _):
        state = apply_split(ends[...], high[i], low[i]) + rows_out[i]
        ends[...] = state
        rows_out[i] = state
        return 0

    lax.fori_loop(0, rows, step, 0)


def behind_body(high, low, source, ends):
    rows = source.shape[0]
    ends[...] = jnp.zeros_like(ends)

    def step(i, _):
        j = rows - 1 - i
        ends[...] = apply_split(source[j] + ends[...], high[j], low[j])
        return 0

    lax.fori_loop(0, rows, step, 0)


def respond_ahead(high, low, prefix, forward):
    rows, count, width = forward.shape
    length = 2 * width + count
    return call(
        ahead_body,
        [shape(rows, length, width), shape(length, width)],
        [],
        2 * rows * 6 * length * width * width,
        high,
        low,
        prefix,
        forward,
    )


def respond_behind(high, low, source, after):
    rows, length, width = source.shape
    return call(
        behind_body,
        [shape(length, width)],
        [],
        rows * 6 * length * width * width,
        high,
        low,
        source,
        after=after,
    )[0]


def identity(width):
    return (
        lax.broadcasted_iota(jnp.int32, (width, width), 0)
        == lax.broadcasted_iota(jnp.int32, (width, width), 1)
    ).astype(jnp.float32)


def row_span(spans, e, part):
    return spans[e, part]


def far_span(spans, e, part):
    return jnp.concatenate([spans[2 * e, part], spans[2 * e + 1, part]], axis=0)


def merge(before, behind):
    width = before[0].shape[0]
    ahead = apply_split(before[0], *split(behind[0]))
    turned = apply_split(before[0], *split(behind[2]))
    back = apply_split(jnp.concatenate([behind[1], turned], axis=0), *split(before[1]))
    return ahead, back[:width], before[2] + back[width:]


def compose_body(place, spans, half, whole):
    parts = spans.shape[1]
    width = spans.shape[2]
    level = [tuple(spans[e, part] for part in range(parts)) for e in range(spans.shape[0])]
    while len(level) > 1:
        level = [merge(*level[i : i + 2]) for i in range(0, len(level), 2)]
    kept = pl.ds(pl.multiple_of(place[1] * (width // 2), width // 2), width // 2)
    for part in range(parts):
        whole[...] = level[0][part]
        half[part] = whole[kept]


def compose(place, spans, after):
    members, parts, width, _ = spans.shape
    return call(
        compose_body,
        [shape(parts, width // 2, width)],
        [pltpu.VMEM((width, width), jnp.float32)],
        members * 6 * 4 * width**3,
        spans,
        after=after,
        position=place,
    )[0]


def reach_body(place, spans, own, reach, crossing):
    members, _, width, _ = spans.shape
    reach[0] = identity(width)
    reach[1] = identity(width)
    chip = place[0]

    def outward(e, _):
        @pl.when(e // 2 == chip)
        def _():
            own[e % 2, 0] = reach[0]

        back = members - 1 - e

        @pl.when(back // 2 == chip)
        def _():
            own[back % 2, 1] = reach[1]

        ahead = reach[0]
        crossing[e] = apply_split(ahead, *split(spans[e, 2]))
        reach[1] = apply_split(reach[1], *split(spans[back, 1]))
        reach[0] = apply_split(ahead, *split(spans[e, 0]))
        return 0

    lax.fori_loop(0, members, outward, 0)
    reach[0] = jnp.zeros((width, width), jnp.float32)

    def inward(i, _):
        e = members - 1 - i

        @pl.when(e // 2 == chip)
        def _():
            own[e % 2, 2] = reach[0]

        reach[0] = apply_split(reach[0], *split(spans[e, 1])) + crossing[e]
        return 0

    lax.fori_loop(0, members, inward, 0)


def reaching(place, spans, after):
    members, parts, width, _ = spans.shape
    return call(
        reach_body,
        [shape(2, parts, width, width)],
        [
            pltpu.VMEM((2, width, width), jnp.float32),
            pltpu.VMEM((members, width, width), jnp.float32),
        ],
        members * 6 * 4 * width**3,
        spans,
        after=after,
        position=place,
    )[0]


def relay(span, ends, states):
    members, length, width = ends.shape
    count = (length - 8) // 2
    state = jnp.zeros((count, width), jnp.float32)
    entered = []
    for e in range(members):
        entered.append(state)
        states[0, e] = state
        end = ends[e, :count]
        state = end if e == 0 else apply_split(state, *split(span(e, 0))) + end
    ahead = state
    state = jnp.zeros((count, width), jnp.float32)
    for e in reversed(range(members)):
        states[1, e] = state
        end = ends[e, count : 2 * count]
        if e > 0:
            end = end + apply_split(entered[e], *split(span(e, 2)))
        state = end if e == members - 1 else apply_split(state, *split(span(e, 1))) + end
    return ahead, state


def total_of(ends):
    count = (ends.shape[1] - 8) // 2
    total = ends[0, 2 * count :]
    for e in range(1, ends.shape[0]):
        total = total + ends[e, 2 * count :]
    return total


def near_body(place, spans, ends, entered, messages, states):
    count = entered.shape[2]
    ahead, behind = relay(functools.partial(row_span, spans), ends, states)
    message = jnp.concatenate([ahead, behind, total_of(ends)], axis=0)
    for member in range(messages.shape[0]):
        messages[member] = message
    for core in range(2):
        for way in range(2):
            entered[core, way] = states[way, 2 * place[0] + core]


def near(place, spans, ends, copies):
    members, length, width = ends.shape
    count = (length - 8) // 2
    return call(
        near_body,
        [shape(2, 2, count, width), shape(copies, length, width)],
        [pltpu.VMEM((2, members, count, width), jnp.float32)],
        members * 6 * 3 * count * width * width,
        spans,
        ends,
        position=place,
    )


def far_body(place, spans, ends, own, inner, mine, theirs, squares, states, entering):
    relay(functools.partial(far_span, spans), ends, states)
    ahead, behind = states[0, place[0]], states[1, place[0]]
    for core in range(2):
        entering[core, 0] = apply_split(ahead, *split(own[core, 0])) + inner[core, 0]
        entering[core, 1] = (
            apply_split(behind, *split(own[core, 1]))
            + apply_split(ahead, *split(own[core, 2]))
            + inner[core, 1]
        )
    mine[...] = entering[place[1]]
    theirs[...] = entering[1 - place[1]]
    squares[...] = total_of(ends)


def far(place, spans, ends, own, inner, after=()):
    members, length, width = ends.shape
    count = (length - 8) // 2
    return call(
        far_body,
        [shape(2, count, width), shape(2, count, width), shape(8, width)],
        [
            pltpu.VMEM((2, members, count, width), jnp.float32),
            pltpu.VMEM((2, 2, count, width), jnp.float32),
        ],
        members * 6 * 3 * count * width * width,
        spans,
        ends,
        own,
        inner,
        after=after,
        position=place,
    )


def both_halves(place, mine, theirs, way):
    first = place[1] == 0
    return jnp.concatenate(
        [
            jnp.where(first, mine[way], theirs[way]),
            jnp.where(first, theirs[way], mine[way]),
        ],
        axis=0,
    )


def put_messages(messages, ahead, behind, sums):
    count = ahead.shape[0] // 2
    for member in range(messages.shape[0]):
        chosen = slice((member % 2) * count, (member % 2 + 1) * count)
        messages[member, :count] = ahead[chosen]
        messages[member, count : 2 * count] = behind[chosen]
        messages[member, 2 * count :] = jnp.zeros((8, messages.shape[2]), jnp.float32)
        if sums is not None:
            messages[member, 2 * count :, : 2 * count] = sums


def row_sums(total):
    ones = jnp.ones((8, total.shape[1]), jnp.float32)
    return lax.dot_general(
        ones,
        total,
        (((1,), (1,)), ((), ())),
        precision=lax.Precision.HIGHEST,
        preferred_element_type=jnp.float32,
    )


def first_body(place, high, low, source, mine, theirs, ahead_ends, behind_ends, solved, messages, forward):
    rows, count, width = source.shape
    entering = [both_halves(place, mine, theirs, way) for way in range(2)]

    def ahead(i, state):
        state = apply_split(state, high[i], low[i]) + source[i]
        forward[i] = state
        return state

    lax.fori_loop(0, rows, ahead, entering[0], unroll=8)

    def behind(i, carry):
        state, total = carry
        j = rows - 1 - i
        state = apply_split(forward[j] + state, high[j], low[j])
        solved[j] = state
        return state, total + state * state

    zero = jnp.zeros((count, width), jnp.float32)
    _, total = lax.fori_loop(0, rows, behind, (entering[1], zero), unroll=8)
    parts = [
        ends[2 * width :]
        + apply_split(entering[0], *split(ends[:width]))
        + apply_split(entering[1], *split(ends[width : 2 * width]))
        for ends in (ahead_ends, behind_ends)
    ]
    put_messages(messages, *parts, row_sums(total))


def first_rows(place, high, low, source, mine, theirs, ahead_ends, behind_ends, copies):
    rows, count, width = source.shape
    return call(
        first_body,
        [shape(*source.shape), shape(copies, count + 8, width)],
        [pltpu.VMEM(source.shape, jnp.float32)],
        2 * rows * 6 * count * width * width,
        high,
        low,
        source,
        mine,
        theirs,
        ahead_ends,
        behind_ends,
        position=place,
    )


def second_body(place, high, low, source, mine, theirs, scale, result, squares, forward):
    rows, count, width = source.shape
    inverse = 1.0 / scale[...]
    entering = [both_halves(place, mine, theirs, way) for way in range(2)]

    def ahead(i, state):
        state = apply_split(state, high[i], low[i]) + source[i]
        forward[i] = state
        return state

    lax.fori_loop(0, rows, ahead, entering[0], unroll=8)

    def behind(i, carry):
        state, total = carry
        j = rows - 1 - i
        state = apply_split(forward[j] + state, high[j], low[j])
        value = state * inverse
        result[j] = value
        return state, total + value * value

    zero = jnp.zeros((count, width), jnp.float32)
    _, total = lax.fori_loop(0, rows, behind, (entering[1], zero), unroll=8)
    squares[...] = jnp.zeros(squares.shape, jnp.float32)
    sums = row_sums(total)
    for member in range(squares.shape[0]):
        squares[member, :, :count] = sums


def second_rows(place, high, low, source, mine, theirs, scale, copies):
    rows, count, width = source.shape
    return call(
        second_body,
        [shape(*source.shape), shape(copies, 8, 128)],
        [pltpu.VMEM(source.shape, jnp.float32)],
        2 * rows * 6 * count * width * width,
        high,
        low,
        source,
        mine,
        theirs,
        scale,
        position=place,
    )


def scale_body(vectors, scale, result):
    result[...] = vectors[...] * (1.0 / scale[...])[None]


def rescale(vectors, scale):
    return call(scale_body, [shape(*vectors.shape)], [], vectors.size, vectors, scale)[0]


def swap(value, axis):
    return lax.all_to_all(value, axis, 0, 0, tiled=True)


def shards(start_vectors, factors):
    rows, count, width = start_vectors.shape
    cell_count = rows * lax.axis_size(CHAIN) * width
    members, groups = lax.axis_size(INNER), lax.axis_size("outer")
    core = lax.axis_index("core")
    near_place = jnp.stack([lax.axis_index("mid"), core]).astype(jnp.int32)
    far_place = jnp.stack([lax.axis_index("outer"), core]).astype(jnp.int32)
    cross_core = functools.partial(lax.ppermute, axis_name="core", perm=[(0, 1), (1, 0)])

    whole = lax.all_gather(factors, "cols", axis=1, tiled=True)
    high, low, prefix, local, operators, ends = prepare(whole, start_vectors, members)
    near_spans = lax.all_gather(operators, INNER)
    near_ends = swap(ends, INNER)
    ahead_rows, ahead_ends = respond_ahead(high, low, prefix, local)
    half = compose(near_place, near_spans, (ahead_ends, near_ends))
    far_spans = lax.all_gather(half, ("outer", "core"))
    inner, message = near(near_place, near_spans, near_ends, groups)
    far_ends = swap(message, "outer")
    behind_ends = respond_behind(high, low, ahead_rows, (half,))
    own = reaching(near_place, near_spans, (half,))
    mine, theirs, _ = far(far_place, far_spans, far_ends, own, inner, (behind_ends,))

    first_solve, message = first_rows(
        near_place,
        high,
        low,
        start_vectors,
        mine,
        cross_core(theirs),
        ahead_ends,
        behind_ends,
        members,
    )
    inner, message = near(near_place, near_spans, swap(message, INNER), groups)
    mine, theirs, squares = far(far_place, far_spans, swap(message, "outer"), own, inner)
    scale_one = jnp.sqrt(squares[0, :count] / cell_count + eps_value)
    second, squares = second_rows(
        near_place, high, low, first_solve, mine, cross_core(theirs), scale_one[:, None], members
    )
    squares = jnp.sum(swap(squares, INNER), axis=0)
    squares = jnp.broadcast_to(squares[None], (groups, *squares.shape))
    squares = jnp.sum(swap(squares, "outer"), axis=0)
    scale_two = jnp.sqrt(squares[0, :count] / cell_count + eps_value)
    return rescale(second, scale_two[:, None]), jnp.log(scale_two)


def solution(mesh):
    size = mesh.shape["chain"]
    outer = 1 << ((size - 1).bit_length() // 2)
    devices = mesh.devices.reshape(outer, size // outer // 2, 2, mesh.shape["cols"])
    placed = P(CHAIN, "cols", None)
    return jax.shard_map(
        shards,
        mesh=Mesh(devices, (*CHAIN, "cols")),
        in_specs=(placed, placed),
        out_specs=(placed, P("cols")),
        check_vma=False,
    )
```

```python
import functools

import jax
import jax.numpy as jnp
from jax import lax
from jax.experimental import pallas as pl
from jax.experimental.pallas import tpu as pltpu
from jax.sharding import Mesh, PartitionSpec as P

eps_value = 1e-06
VMEM_BYTES = 56 * 1024 * 1024
INNER = ("mid", "core")
CHAIN = ("outer", *INNER)


def split(value):
    high = value.astype(jnp.bfloat16)
    low = (value - high.astype(jnp.float32)).astype(jnp.bfloat16)
    return high, low


def apply_split(state, high, low):
    rows = state.shape[0]
    state_high, state_low = split(state)
    both = jnp.dot(
        jnp.concatenate([state_high, state_low], axis=0),
        high,
        preferred_element_type=jnp.float32,
    )
    return (both[:rows] + both[rows:]) + jnp.dot(
        state_high, low, preferred_element_type=jnp.float32
    )


def call(body, out_shapes, scratch, flops, *operands, after=(), position=None):
    vmem = pl.BlockSpec(memory_space=pltpu.VMEM)
    touched = sum(x.size * x.dtype.itemsize for x in (*operands, *out_shapes))
    specs = [vmem] * len(operands)
    if position is not None:
        specs = [pl.BlockSpec(memory_space=pltpu.SMEM), *specs]
        operands = (position, *operands)
    kernel = body
    if after:
        specs = [pl.BlockSpec(memory_space=pl.ANY)] * len(after) + specs
        operands = (*after, *operands)

        def kernel(*refs):
            body(*refs[len(after) :])

    return pl.pallas_call(
        kernel,
        out_shape=tuple(out_shapes),
        in_specs=specs,
        out_specs=tuple([vmem] * len(out_shapes)),
        scratch_shapes=scratch,
        compiler_params=pltpu.CompilerParams(vmem_limit_bytes=VMEM_BYTES),
        cost_estimate=pl.CostEstimate(flops=flops, bytes_accessed=touched, transcendentals=0),
    )(*operands)


def shape(*dims, dtype=jnp.float32):
    return jax.ShapeDtypeStruct(dims, dtype)


def prepare_body(factors, source, high, low, prefix, forward, operators, ends, ahead, back, behind):
    rows, width, _ = factors.shape
    count = source.shape[1]
    ahead[:count] = jnp.zeros((count, width), jnp.float32)
    ahead[count:] = identity(width)
    behind[...] = jnp.zeros_like(behind)
    back[0], back[1] = split(identity(width))

    def step(i, _):
        turned = split(factors[i].T)
        high[i], low[i] = turned
        both = jnp.dot(
            jnp.concatenate(turned, axis=0), back[0], preferred_element_type=jnp.float32
        )
        through = (both[:width] + both[width:]) + jnp.dot(
            turned[0], back[1], preferred_element_type=jnp.float32
        )
        moved = apply_split(ahead[...], *turned)
        state = moved[:count] + source[i]
        forward[i] = state
        prefix[i] = moved[count:]
        ahead[:count] = state
        ahead[count:] = moved[count:]
        back[0], back[1] = split(through)
        operators[1] = through
        behind[...] += apply_split(ahead[...], back[0], back[1])
        return 0

    lax.fori_loop(0, rows, step, 0, unroll=8)
    operators[0] = ahead[count:]
    operators[2] = behind[count:]
    put_messages(ends, ahead[:count], behind[:count], None)


def prepare(factors, source, copies):
    rows, width, _ = factors.shape
    count = source.shape[1]
    square = (rows, width, width)
    return call(
        prepare_body,
        [
            shape(*square, dtype=jnp.bfloat16),
            shape(*square, dtype=jnp.bfloat16),
            shape(*square),
            shape(*source.shape),
            shape(3, width, width),
            shape(copies, count + 8, width),
        ],
        [
            pltpu.VMEM((count + width, width), jnp.float32),
            pltpu.VMEM((2, width, width), jnp.bfloat16),
            pltpu.VMEM((count + width, width), jnp.float32),
        ],
        rows * 6 * (2 * count + 3 * width) * width * width,
        factors,
        source,
    )


def ahead_body(high, low, prefix, forward, rows_out, ends):
    rows, count, width = forward.shape
    zero = jnp.zeros((width, width), jnp.float32)
    ends[:width] = zero
    ends[width : 2 * width] = identity(width)
    ends[2 * width :] = jnp.zeros((count, width), jnp.float32)

    def back(i, _):
        j = rows - 1 - i
        source = jnp.concatenate([prefix[j], zero, forward[j]], axis=0)
        state = apply_split(source + ends[...], high[j], low[j])
        ends[...] = state
        rows_out[j] = state
        return 0

    lax.fori_loop(0, rows, back, 0)
    ends[...] = jnp.zeros_like(ends)

    def step(i, _):
        state = apply_split(ends[...], high[i], low[i]) + rows_out[i]
        ends[...] = state
        rows_out[i] = state
        return 0

    lax.fori_loop(0, rows, step, 0)


def behind_body(high, low, source, ends):
    rows = source.shape[0]
    ends[...] = jnp.zeros_like(ends)

    def step(i, _):
        j = rows - 1 - i
        ends[...] = apply_split(source[j] + ends[...], high[j], low[j])
        return 0

    lax.fori_loop(0, rows, step, 0)


def respond_ahead(high, low, prefix, forward):
    rows, count, width = forward.shape
    length = 2 * width + count
    return call(
        ahead_body,
        [shape(rows, length, width), shape(length, width)],
        [],
        2 * rows * 6 * length * width * width,
        high,
        low,
        prefix,
        forward,
    )


def respond_behind(high, low, source, after):
    rows, length, width = source.shape
    return call(
        behind_body,
        [shape(length, width)],
        [],
        rows * 6 * length * width * width,
        high,
        low,
        source,
        after=after,
    )[0]


def identity(width):
    return (
        lax.broadcasted_iota(jnp.int32, (width, width), 0)
        == lax.broadcasted_iota(jnp.int32, (width, width), 1)
    ).astype(jnp.float32)


def row_span(spans, e, part):
    return spans[e, part]


def far_span(spans, e, part):
    return jnp.concatenate([spans[2 * e, part], spans[2 * e + 1, part]], axis=0)


def merge(before, behind):
    width = before[0].shape[0]
    ahead = apply_split(before[0], *split(behind[0]))
    turned = apply_split(before[0], *split(behind[2]))
    back = apply_split(jnp.concatenate([behind[1], turned], axis=0), *split(before[1]))
    return ahead, back[:width], before[2] + back[width:]


def compose_body(place, spans, half, whole):
    parts = spans.shape[1]
    width = spans.shape[2]
    level = [tuple(spans[e, part] for part in range(parts)) for e in range(spans.shape[0])]
    while len(level) > 1:
        level = [merge(*level[i : i + 2]) for i in range(0, len(level), 2)]
    kept = pl.ds(pl.multiple_of(place[1] * (width // 2), width // 2), width // 2)
    for part in range(parts):
        whole[...] = level[0][part]
        half[part] = whole[kept]


def compose(place, spans, after):
    members, parts, width, _ = spans.shape
    return call(
        compose_body,
        [shape(parts, width // 2, width)],
        [pltpu.VMEM((width, width), jnp.float32)],
        members * 6 * 4 * width**3,
        spans,
        after=after,
        position=place,
    )[0]


def reach_body(place, spans, own, reach, crossing):
    members, _, width, _ = spans.shape
    reach[0] = identity(width)
    reach[1] = identity(width)
    chip = place[0]

    def outward(e, _):
        @pl.when(e // 2 == chip)
        def _():
            own[e % 2, 0] = reach[0]

        back = members - 1 - e

        @pl.when(back // 2 == chip)
        def _():
            own[back % 2, 1] = reach[1]

        ahead = reach[0]
        crossing[e] = apply_split(ahead, *split(spans[e, 2]))
        reach[1] = apply_split(reach[1], *split(spans[back, 1]))
        reach[0] = apply_split(ahead, *split(spans[e, 0]))
        return 0

    lax.fori_loop(0, members, outward, 0)
    reach[0] = jnp.zeros((width, width), jnp.float32)

    def inward(i, _):
        e = members - 1 - i

        @pl.when(e // 2 == chip)
        def _():
            own[e % 2, 2] = reach[0]

        reach[0] = apply_split(reach[0], *split(spans[e, 1])) + crossing[e]
        return 0

    lax.fori_loop(0, members, inward, 0)


def reaching(place, spans, after):
    members, parts, width, _ = spans.shape
    return call(
        reach_body,
        [shape(2, parts, width, width)],
        [
            pltpu.VMEM((2, width, width), jnp.float32),
            pltpu.VMEM((members, width, width), jnp.float32),
        ],
        members * 6 * 4 * width**3,
        spans,
        after=after,
        position=place,
    )[0]


def relay(span, ends, states):
    members, length, width = ends.shape
    count = (length - 8) // 2
    state = jnp.zeros((count, width), jnp.float32)
    entered = []
    for e in range(members):
        entered.append(state)
        states[0, e] = state
        end = ends[e, :count]
        state = end if e == 0 else apply_split(state, *split(span(e, 0))) + end
    ahead = state
    state = jnp.zeros((count, width), jnp.float32)
    for e in reversed(range(members)):
        states[1, e] = state
        end = ends[e, count : 2 * count]
        if e > 0:
            end = end + apply_split(entered[e], *split(span(e, 2)))
        state = end if e == members - 1 else apply_split(state, *split(span(e, 1))) + end
    return ahead, state


def total_of(ends):
    count = (ends.shape[1] - 8) // 2
    total = ends[0, 2 * count :]
    for e in range(1, ends.shape[0]):
        total = total + ends[e, 2 * count :]
    return total


def near_body(place, spans, ends, entered, messages, states):
    count = entered.shape[2]
    ahead, behind = relay(functools.partial(row_span, spans), ends, states)
    message = jnp.concatenate([ahead, behind, total_of(ends)], axis=0)
    for member in range(messages.shape[0]):
        messages[member] = message
    for core in range(2):
        for way in range(2):
            entered[core, way] = states[way, 2 * place[0] + core]


def near(place, spans, ends, copies):
    members, length, width = ends.shape
    count = (length - 8) // 2
    return call(
        near_body,
        [shape(2, 2, count, width), shape(copies, length, width)],
        [pltpu.VMEM((2, members, count, width), jnp.float32)],
        members * 6 * 3 * count * width * width,
        spans,
        ends,
        position=place,
    )


def far_body(place, spans, ends, own, inner, mine, theirs, squares, states, entering):
    relay(functools.partial(far_span, spans), ends, states)
    ahead, behind = states[0, place[0]], states[1, place[0]]
    for core in range(2):
        entering[core, 0] = apply_split(ahead, *split(own[core, 0])) + inner[core, 0]
        entering[core, 1] = (
            apply_split(behind, *split(own[core, 1]))
            + apply_split(ahead, *split(own[core, 2]))
            + inner[core, 1]
        )
    mine[...] = entering[place[1]]
    theirs[...] = entering[1 - place[1]]
    squares[...] = total_of(ends)


def far(place, spans, ends, own, inner, after=()):
    members, length, width = ends.shape
    count = (length - 8) // 2
    return call(
        far_body,
        [shape(2, count, width), shape(2, count, width), shape(8, width)],
        [
            pltpu.VMEM((2, members, count, width), jnp.float32),
            pltpu.VMEM((2, 2, count, width), jnp.float32),
        ],
        members * 6 * 3 * count * width * width,
        spans,
        ends,
        own,
        inner,
        after=after,
        position=place,
    )


def both_halves(place, mine, theirs, way):
    first = place[1] == 0
    return jnp.concatenate(
        [
            jnp.where(first, mine[way], theirs[way]),
            jnp.where(first, theirs[way], mine[way]),
        ],
        axis=0,
    )


def put_messages(messages, ahead, behind, sums):
    count = ahead.shape[0] // 2
    for member in range(messages.shape[0]):
        chosen = slice((member % 2) * count, (member % 2 + 1) * count)
        messages[member, :count] = ahead[chosen]
        messages[member, count : 2 * count] = behind[chosen]
        messages[member, 2 * count :] = jnp.zeros((8, messages.shape[2]), jnp.float32)
        if sums is not None:
            messages[member, 2 * count :, : 2 * count] = sums


def row_sums(total):
    ones = jnp.ones((8, total.shape[1]), jnp.float32)
    return lax.dot_general(
        ones,
        total,
        (((1,), (1,)), ((), ())),
        precision=lax.Precision.HIGHEST,
        preferred_element_type=jnp.float32,
    )


def first_body(place, high, low, source, mine, theirs, ahead_ends, behind_ends, solved, messages, forward):
    rows, count, width = source.shape
    entering = [both_halves(place, mine, theirs, way) for way in range(2)]

    def ahead(i, state):
        state = apply_split(state, high[i], low[i]) + source[i]
        forward[i] = state
        return state

    lax.fori_loop(0, rows, ahead, entering[0], unroll=8)

    def behind(i, carry):
        state, total = carry
        j = rows - 1 - i
        state = apply_split(forward[j] + state, high[j], low[j])
        solved[j] = state
        return state, total + state * state

    zero = jnp.zeros((count, width), jnp.float32)
    _, total = lax.fori_loop(0, rows, behind, (entering[1], zero), unroll=8)
    parts = [
        ends[2 * width :]
        + apply_split(entering[0], *split(ends[:width]))
        + apply_split(entering[1], *split(ends[width : 2 * width]))
        for ends in (ahead_ends, behind_ends)
    ]
    put_messages(messages, *parts, row_sums(total))


def first_rows(place, high, low, source, mine, theirs, ahead_ends, behind_ends, copies):
    rows, count, width = source.shape
    return call(
        first_body,
        [shape(*source.shape), shape(copies, count + 8, width)],
        [pltpu.VMEM(source.shape, jnp.float32)],
        2 * rows * 6 * count * width * width,
        high,
        low,
        source,
        mine,
        theirs,
        ahead_ends,
        behind_ends,
        position=place,
    )


def second_body(cell_count, place, high, low, source, mine, theirs, first_squares, result, squares, forward):
    rows, count, width = source.shape
    inverse = 1.0 / upright(scale_of(first_squares[:1, :count], cell_count))
    entering = [both_halves(place, mine, theirs, way) for way in range(2)]

    def ahead(i, state):
        state = apply_split(state, high[i], low[i]) + source[i]
        forward[i] = state
        return state

    lax.fori_loop(0, rows, ahead, entering[0], unroll=8)

    def behind(i, carry):
        state, total = carry
        j = rows - 1 - i
        state = apply_split(forward[j] + state, high[j], low[j])
        value = state * inverse
        result[j] = value
        return state, total + value * value

    zero = jnp.zeros((count, width), jnp.float32)
    _, total = lax.fori_loop(0, rows, behind, (entering[1], zero), unroll=8)
    squares[...] = jnp.zeros(squares.shape, jnp.float32)
    sums = row_sums(total)
    for member in range(squares.shape[0]):
        squares[member, :, :count] = sums


def second_rows(place, high, low, source, mine, theirs, first_squares, cell_count, copies):
    rows, count, width = source.shape
    return call(
        functools.partial(second_body, cell_count),
        [shape(*source.shape), shape(copies, 8, 128)],
        [pltpu.VMEM(source.shape, jnp.float32)],
        2 * rows * 6 * count * width * width,
        high,
        low,
        source,
        mine,
        theirs,
        first_squares,
        position=place,
    )


def scale_of(squares, cell_count):
    return jnp.sqrt(squares / cell_count + eps_value)


def upright(row):
    size = row.shape[1]
    mine = lax.broadcasted_iota(jnp.int32, (size, size), 0) == lax.broadcasted_iota(
        jnp.int32, (size, size), 1
    )
    spread = jnp.where(mine, jnp.broadcast_to(row, (size, size)), 0.0)
    return jnp.sum(spread, axis=1, keepdims=True)


def scale_body(cell_count, vectors, squares, result, growth):
    count = vectors.shape[1]
    total = squares[0]
    for group in range(1, squares.shape[0]):
        total = total + squares[group]
    scale = scale_of(total, cell_count)
    result[...] = vectors[...] * (1.0 / upright(scale[:1, :count]))[None]
    growth[...] = jnp.log(scale)


def rescale(vectors, squares, cell_count):
    return call(
        functools.partial(scale_body, cell_count),
        [shape(*vectors.shape), shape(*squares.shape[1:])],
        [],
        vectors.size,
        vectors,
        squares,
    )


def swap(value, axis):
    return lax.all_to_all(value, axis, 0, 0, tiled=True)


def shards(start_vectors, factors):
    rows, count, width = start_vectors.shape
    cell_count = rows * lax.axis_size(CHAIN) * width
    members, groups = lax.axis_size(INNER), lax.axis_size("outer")
    core = lax.axis_index("core")
    near_place = jnp.stack([lax.axis_index("mid"), core]).astype(jnp.int32)
    far_place = jnp.stack([lax.axis_index("outer"), core]).astype(jnp.int32)
    cross_core = functools.partial(lax.ppermute, axis_name="core", perm=[(0, 1), (1, 0)])

    whole = lax.all_gather(factors, "cols", axis=1, tiled=True)
    high, low, prefix, local, operators, ends = prepare(whole, start_vectors, members)
    near_spans = lax.all_gather(operators, INNER)
    near_ends = swap(ends, INNER)
    ahead_rows, ahead_ends = respond_ahead(high, low, prefix, local)
    half = compose(near_place, near_spans, (ahead_ends, near_ends))
    far_spans = lax.all_gather(half, ("outer", "core"))
    inner, message = near(near_place, near_spans, near_ends, groups)
    far_ends = swap(message, "outer")
    behind_ends = respond_behind(high, low, ahead_rows, (half,))
    own = reaching(near_place, near_spans, (half,))
    mine, theirs, _ = far(far_place, far_spans, far_ends, own, inner, (behind_ends,))

    first_solve, message = first_rows(
        near_place,
        high,
        low,
        start_vectors,
        mine,
        cross_core(theirs),
        ahead_ends,
        behind_ends,
        members,
    )
    inner, message = near(near_place, near_spans, swap(message, INNER), groups)
    mine, theirs, squares = far(far_place, far_spans, swap(message, "outer"), own, inner)
    second, squares = second_rows(
        near_place, high, low, first_solve, mine, cross_core(theirs), squares, cell_count, members
    )
    squares = jnp.sum(swap(squares, INNER), axis=0)
    squares = jnp.broadcast_to(squares[None], (groups, *squares.shape))
    vectors, growth = rescale(second, swap(squares, "outer"), cell_count)
    return vectors, growth[0, :count]


def solution(mesh):
    size = mesh.shape["chain"]
    outer = 1 << ((size - 1).bit_length() // 2)
    devices = mesh.devices.reshape(outer, size // outer // 2, 2, mesh.shape["cols"])
    placed = P(CHAIN, "cols", None)
    return jax.shard_map(
        shards,
        mesh=Mesh(devices, (*CHAIN, "cols")),
        in_specs=(placed, placed),
        out_specs=(placed, P("cols")),
        check_vma=False,
    )
```
